32 devices in a mesh: seq: 16 (over z, y, x), mdl: 2 (over core).
Axes of the slice: x: 2, y: 2, z: 4, core: 2. Of those that a mesh axis runs over, the one named last changes fastest.
Arguments:
- hidden_in: bfloat16 [32, 4, 2048], P(None, None, 'seq'), may hold values from -25 to 25
- cache_keys: bfloat16 [32, 512, 2048], P(None, 'seq', 'mdl'), may hold values from -250 to 250, as said below
- cache_values: bfloat16 [32, 512, 2048], P(None, 'seq', 'mdl'), may hold values from -6 to 6
- lengths: int32 [32], replicated, may hold values from 1 to 508, as said below
- query_weight: bfloat16 [2048, 2048], P('seq', 'mdl'), may hold values from -0.125 to 0.125
- key_weight: bfloat16 [2048, 2048], P('seq', 'mdl'), may hold values from -0.125 to 0.125
- value_weight: bfloat16 [2048, 2048], P('seq', 'mdl'), may hold values from -0.125 to 0.125
- out_weight: bfloat16 [2048, 2048], P('mdl', 'seq'), may hold values from -0.125 to 0.125
- gate_weight: bfloat16 [2048, 8192], P('seq', 'mdl'), may hold values from -0.125 to 0.125
- up_weight: bfloat16 [2048, 8192], P('seq', 'mdl'), may hold values from -0.125 to 0.125
- down_weight: bfloat16 [8192, 2048], P('mdl', 'seq'), may hold values from -0.0625 to 0.0625
Outputs:
- hidden_out: bfloat16 [32, 4, 2048], P(None, None, 'seq')
- new_cache_keys: bfloat16 [32, 512, 2048], P(None, 'seq', 'mdl')
- new_cache_values: bfloat16 [32, 512, 2048], P(None, 'seq', 'mdl')
The draws below stay inside these ranges and needn't reach their ends.
Inputs may be any that keep to these rules, and one draw needn't show every extreme that they name: `cache_keys`: keys are stored after their rotary embedding. `lengths`: at least one request has exactly 508 cached positions.
All inputs are finite; a program needn't handle non-finite values.
Results may differ from the reference program's by a relative error of at most 0.012.
The reference program's roundings to bfloat16 on the way (of `normed`, `attended`, `normed2` and `act`) count: a program that leaves them out, or rounds other values in their place, can miss the bound.
Values may be sent and summed in bfloat16 or wider, within the bound.
A program may use at most 64 MiB of HBM per device.

```python
import jax
import jax.numpy as jnp
from jax import lax

D = 2048
HEADS = 16
FF = 8192
HEAD_DIM = 128
REQ = 32
NEW = 4
MAXLEN = 512


def draw_hidden_in(key, part):
    parts_keys = jax.random.split(key, 2)
    column = jnp.arange(D, dtype=jnp.float32) / D
    row_scale = jnp.exp(jax.random.uniform(parts_keys[0], (REQ, NEW, 1), jnp.float32, jnp.log(0.2), jnp.log(2.0)))
    column_scale = 0.5 * jnp.exp(jnp.log(3.0) * column)
    entries = jnp.clip(jax.random.normal(parts_keys[1], (REQ, NEW, D), jnp.float32), -6.0, 6.0)
    return (row_scale * column_scale * entries).astype(jnp.bfloat16)


def draw_cache_keys(key, part):
    parts_keys = jax.random.split(key, 1)
    entries = jnp.clip(jax.random.normal(parts_keys[0], (REQ, MAXLEN, D), jnp.float32), -6.0, 6.0)
    return (3.0 * entries).astype(jnp.bfloat16)


def draw_lengths(key, part):
    parts_keys = jax.random.split(key, 4)
    longest = MAXLEN - NEW
    first_draw = jax.random.randint(parts_keys[0], (REQ,), 0, longest)
    second_draw = jax.random.randint(parts_keys[1], (REQ,), 0, longest)
    shifts = jax.random.randint(parts_keys[2], (REQ,), 0, 3)
    drawn = 1 + jnp.right_shift(first_draw * second_draw // longest, shifts)
    chosen = jax.random.randint(parts_keys[3], (), 0, REQ)
    return jnp.where(jnp.arange(REQ) == chosen, longest, drawn).astype(jnp.int32)


def steps_of(key, shape, cuts, smallest, largest):
    def one(position, blocks):
        draws = jax.random.uniform(jax.random.fold_in(jax.random.fold_in(key, 6), position), (blocks,), jnp.float32, smallest / len(cuts), largest / len(cuts))
        return jnp.repeat(jnp.exp(draws), shape[position] // blocks).reshape((-1,) + (1,) * (len(shape) - position - 1))

    factor_of = one(*cuts[0])
    for cut in cuts[1:]:
        factor_of = factor_of * one(*cut)
    return factor_of


def centred(stream_key, shape, width, reach, pieces=(), held_as=jnp.bfloat16):
    values = width * jax.random.normal(stream_key, shape, jnp.float32)
    if pieces:
        values = values * steps_of(stream_key, shape, pieces, -0.22, 0.18)
    return jnp.clip(values, -reach, reach).astype(held_as)


def setup_inputs(seed: int = 0) -> dict:
    streams_of = jax.random.split(jax.random.key(seed), 12)
    return {
        "hidden_in": draw_hidden_in(jax.random.fold_in(streams_of[11], 71), 0),
        "cache_keys": draw_cache_keys(jax.random.fold_in(streams_of[11], 71), 0),
        "cache_values": centred(streams_of[2], (REQ, MAXLEN, D), 1.0, 6.0, ((1, 16), (2, 2))),
        "lengths": draw_lengths(jax.random.fold_in(streams_of[11], 71), 0),
        "query_weight": centred(streams_of[4], (D, D), D ** -0.5, 0.125, ((0, 16), (1, 2))),
        "key_weight": centred(streams_of[5], (D, D), D ** -0.5, 0.125, ((0, 16), (1, 2))),
        "value_weight": centred(streams_of[6], (D, D), D ** -0.5, 0.125, ((0, 16), (1, 2))),
        "out_weight": centred(streams_of[7], (D, D), D ** -0.5, 0.125, ((0, 2), (1, 16))),
        "gate_weight": centred(streams_of[8], (D, FF), D ** -0.5, 0.125, ((0, 16), (1, 2))),
        "up_weight": centred(streams_of[9], (D, FF), D ** -0.5, 0.125, ((0, 16), (1, 2))),
        "down_weight": centred(streams_of[10], (FF, D), FF ** -0.5, 0.0625, ((0, 2), (1, 16))),
    }


EPS = 1e-05
THETA = 10000.0
NEGATIVE = -1e+30

def layer_norm(row_block):
    row_mean = lax.optimization_barrier(jnp.mean(row_block, axis=-1, keepdims=True))
    second_moment = lax.optimization_barrier(jnp.mean(row_block * row_block, axis=-1, keepdims=True))
    return (row_block - row_mean) / jnp.sqrt(second_moment - row_mean * row_mean + EPS)

def rotate(vectors, placed_pos):
    half_dim = HEAD_DIM // 2
    freqs = THETA ** (-jnp.arange(half_dim, dtype=jnp.float32) * 2.0 / HEAD_DIM)
    angles = placed_pos.astype(jnp.float32)[..., None, None] * freqs
    cosine = jnp.cos(angles)
    sine = jnp.sin(angles)
    first_half = vectors[..., :half_dim]
    second_half = vectors[..., half_dim:]
    return jnp.concatenate([first_half * cosine - second_half * sine, second_half * cosine + first_half * sine], axis=-1)

def reference(hidden_in, cache_keys, cache_values, lengths, query_weight, key_weight, value_weight, out_weight, gate_weight, up_weight, down_weight):
    widened = hidden_in.astype(jnp.float32)
    normed = layer_norm(widened).astype(jnp.bfloat16).reshape(REQ * NEW, D)
    queries = jnp.dot(normed, query_weight, preferred_element_type=jnp.float32).reshape(REQ, NEW, HEADS, HEAD_DIM)
    new_keys = jnp.dot(normed, key_weight, preferred_element_type=jnp.float32).reshape(REQ, NEW, HEADS, HEAD_DIM)
    new_values = jnp.dot(normed, value_weight, preferred_element_type=jnp.float32).reshape(REQ, NEW, HEADS, HEAD_DIM)
    positions = lengths[:, None] + jnp.arange(NEW, dtype=jnp.int32)[None, :]
    rot_queries = rotate(queries, positions).astype(jnp.bfloat16)
    new_keys = rotate(new_keys, positions).astype(jnp.bfloat16)
    new_values = new_values.astype(jnp.bfloat16)
    score_scale = 1.0 / jnp.sqrt(jnp.float32(HEAD_DIM))

    def attend(items):
        query_rows, key_rows, value_rows, old_keys, old_values, length_one = items
        query_rows = query_rows.astype(jnp.float32)
        old_keys = old_keys.reshape(MAXLEN, HEADS, HEAD_DIM).astype(jnp.float32)
        old_values = old_values.reshape(MAXLEN, HEADS, HEAD_DIM).astype(jnp.float32)
        old_scores = jnp.einsum('thd,jhd->thj', query_rows, old_keys, precision=lax.Precision.HIGHEST) * score_scale
        slot_ids = jnp.arange(MAXLEN, dtype=jnp.int32)
        old_scores = jnp.where(slot_ids[None, None, :] < length_one, old_scores, NEGATIVE)
        new_scores = jnp.einsum('thd,shd->ths', query_rows, key_rows.astype(jnp.float32), precision=lax.Precision.HIGHEST) * score_scale
        token_ids = jnp.arange(NEW, dtype=jnp.int32)
        new_scores = jnp.where(token_ids[None, None, :] <= token_ids[:, None, None], new_scores, NEGATIVE)
        top_score = jnp.maximum(lax.optimization_barrier(jnp.max(old_scores, axis=-1)), lax.optimization_barrier(jnp.max(new_scores, axis=-1)))
        old_weights = jnp.exp(old_scores - top_score[..., None])
        new_weights = jnp.exp(new_scores - top_score[..., None])
        running = lax.optimization_barrier(jnp.sum(old_weights, axis=-1)) + lax.optimization_barrier(jnp.sum(new_weights, axis=-1))
        summed = jnp.einsum('thj,jhd->thd', old_weights, old_values, precision=lax.Precision.HIGHEST)
        summed = summed + jnp.einsum('ths,shd->thd', new_weights, value_rows.astype(jnp.float32), precision=lax.Precision.HIGHEST)
        return (summed / running[..., None]).reshape(NEW, D)
    attended = lax.map(attend, (rot_queries, new_keys, new_values, cache_keys, cache_values, lengths)).astype(jnp.bfloat16)
    mixed = widened + jnp.dot(attended.reshape(REQ * NEW, D), out_weight, preferred_element_type=jnp.float32).reshape(REQ, NEW, D)
    normed2 = layer_norm(mixed).astype(jnp.bfloat16).reshape(REQ * NEW, D)
    gate = jnp.dot(normed2, gate_weight, preferred_element_type=jnp.float32)
    up_rows = jnp.dot(normed2, up_weight, preferred_element_type=jnp.float32)
    act = (jax.nn.silu(gate) * up_rows).astype(jnp.bfloat16)
    hidden_out = (mixed + jnp.dot(act, down_weight, preferred_element_type=jnp.float32).reshape(REQ, NEW, D)).astype(jnp.bfloat16)

    def write_rows(cache_one, rows_one, start_one):
        return lax.dynamic_update_slice(cache_one, rows_one, (start_one.astype(jnp.int32), jnp.int32(0)))
    new_cache_keys = jax.vmap(write_rows)(cache_keys, new_keys.reshape(REQ, NEW, D), lengths)
    new_cache_values = jax.vmap(write_rows)(cache_values, new_values.reshape(REQ, NEW, D), lengths)
    return (hidden_out, new_cache_keys, new_cache_values)
```

```python
import math

import jax
import jax.numpy as jnp
from jax import lax
from jax.sharding import PartitionSpec as P

D = 2048
HEADS = 16


EPS = 1e-05
THETA = 10000.0
NEGATIVE = -1e30


def rotate(vectors, placed_pos):
    head_size = vectors.shape[-1]
    half_dim = head_size // 2
    freqs = THETA ** (-jnp.arange(half_dim, dtype=jnp.float32) * 2.0 / head_size)
    angles = placed_pos.astype(jnp.float32)[..., None, None] * freqs
    cosine = jnp.cos(angles)
    sine = jnp.sin(angles)
    first_half = vectors[..., :half_dim]
    second_half = vectors[..., half_dim:]
    return jnp.concatenate(
        [first_half * cosine - second_half * sine, second_half * cosine + first_half * sine],
        axis=-1,
    )


def normalize(widened, row_sums, square_sums):
    row_mean = row_sums / D
    second_moment = square_sums / D
    inverse = 1.0 / jnp.sqrt(second_moment - row_mean * row_mean + EPS)
    return ((widened - row_mean[..., None]) * inverse[..., None]).astype(jnp.bfloat16)


def body(
    hidden_in,
    cache_keys,
    cache_values,
    lengths,
    query_weight,
    key_weight,
    value_weight,
    out_weight,
    gate_weight,
    up_weight,
    down_weight,
):
    requests, token_count, narrow_width = hidden_in.shape
    slot_count = cache_keys.shape[1]
    local_width = cache_keys.shape[2]
    head_size = D // HEADS
    local_heads = local_width // head_size
    score_scale = 1.0 / math.sqrt(head_size)
    shard_index = lax.axis_index("seq")
    slot_ids = shard_index * slot_count + jnp.arange(slot_count, dtype=jnp.int32)
    live_slots = slot_ids[None, :] < lengths[:, None]
    old_keys = cache_keys.reshape(requests, slot_count, local_heads, head_size)
    old_values = cache_values.reshape(requests, slot_count, local_heads, head_size).astype(
        jnp.float32
    )
    positions = lengths[:, None] + jnp.arange(token_count, dtype=jnp.int32)[None, :]
    out_list = []
    key_list = []
    value_list = []
    for token_step in range(1):
        row_block = hidden_in
        block_rows = row_block.shape[1]
        widened = row_block.astype(jnp.float32)
        row_sums, square_sums = lax.psum(
            (jnp.sum(widened, axis=-1), jnp.sum(widened * widened, axis=-1)), "seq"
        )
        normed = normalize(widened, row_sums, square_sums)
        query_part = jnp.einsum(
            "rnc,cm->rnm", normed, query_weight, preferred_element_type=jnp.float32
        )
        key_part = jnp.einsum("rnc,cm->rnm", normed, key_weight, preferred_element_type=jnp.float32)
        value_part = jnp.einsum(
            "rnc,cm->rnm", normed, value_weight, preferred_element_type=jnp.float32
        )
        queries, keys_full, values_full = lax.psum((query_part, key_part, value_part), "seq")
        placed_pos = positions[:, token_step : token_step + block_rows]
        queries = rotate(
            queries.reshape(requests, block_rows, local_heads, head_size), placed_pos
        ).astype(jnp.bfloat16)
        new_key = rotate(
            keys_full.reshape(requests, block_rows, local_heads, head_size), placed_pos
        ).astype(jnp.bfloat16)
        new_value = values_full.reshape(requests, block_rows, local_heads, head_size).astype(
            jnp.bfloat16
        )
        keys_new = jnp.concatenate(key_list + [new_key], axis=1)
        values_new = jnp.concatenate(value_list + [new_value], axis=1)
        old_scores = (
            jnp.einsum("rnhd,rjhd->rnhj", queries, old_keys, preferred_element_type=jnp.float32)
            * score_scale
        )
        old_scores = jnp.where(live_slots[:, None, None, :], old_scores, NEGATIVE)
        top_old = jnp.max(old_scores, axis=-1)
        weights_old = jnp.where(
            live_slots[:, None, None, :], jnp.exp(old_scores - top_old[..., None]), 0.0
        )
        total_old = jnp.sum(weights_old, axis=-1)
        summed_old = jnp.einsum(
            "rnhj,rjhd->rnhd", weights_old, old_values, precision=lax.Precision.HIGHEST
        )
        top_cache = lax.pmax(top_old, "seq")
        factor_old = jnp.exp(top_old - top_cache)
        total_cache, summed_cache = lax.psum(
            (total_old * factor_old, summed_old * factor_old[..., None]), "seq"
        )
        new_scores = (
            jnp.einsum("rnhd,rshd->rnhs", queries, keys_new, preferred_element_type=jnp.float32)
            * score_scale
        )
        key_index = jnp.arange(keys_new.shape[1], dtype=jnp.int32)
        query_index = token_step + jnp.arange(block_rows, dtype=jnp.int32)
        allowed = key_index[None, :] <= query_index[:, None]
        new_scores = jnp.where(allowed[None, :, None, :], new_scores, NEGATIVE)
        top_new = jnp.max(new_scores, axis=-1)
        weights_new = jnp.exp(new_scores - top_new[..., None])
        total_new = jnp.sum(weights_new, axis=-1)
        summed_new = jnp.einsum(
            "rnhs,rshd->rnhd",
            weights_new,
            values_new.astype(jnp.float32),
            precision=lax.Precision.HIGHEST,
        )
        top_score = jnp.maximum(top_cache, top_new)
        factor_cache = jnp.exp(top_cache - top_score)
        factor_new = jnp.exp(top_new - top_score)
        running = total_cache * factor_cache + total_new * factor_new
        combined = summed_cache * factor_cache[..., None] + summed_new * factor_new[..., None]
        attended = (
            (combined / running[..., None])
            .astype(jnp.bfloat16)
            .reshape(requests, block_rows, local_width)
        )
        attn_part = jnp.einsum(
            "rnm,mc->rnc", attended, out_weight, preferred_element_type=jnp.float32
        )
        mixed = widened + lax.psum(attn_part, "mdl")
        sums_mixed, squares_mixed = lax.psum(
            (jnp.sum(mixed, axis=-1), jnp.sum(mixed * mixed, axis=-1)), "seq"
        )
        normed2 = normalize(mixed, sums_mixed, squares_mixed)
        gate_part = jnp.einsum(
            "rnc,cf->rnf", normed2, gate_weight, preferred_element_type=jnp.float32
        )
        up_part = jnp.einsum("rnc,cf->rnf", normed2, up_weight, preferred_element_type=jnp.float32)
        gate_full, up_full = lax.psum((gate_part, up_part), "seq")
        act_full = (jax.nn.silu(gate_full) * up_full).astype(jnp.bfloat16)
        down_part = jnp.einsum(
            "rnf,fc->rnc", act_full, down_weight, preferred_element_type=jnp.float32
        )
        block_out = (mixed + lax.psum(down_part, "mdl")).astype(jnp.bfloat16)
        block_out, new_key, new_value = (block_out, new_key, new_value)
        out_list.append(block_out)
        key_list.append(new_key)
        value_list.append(new_value)
    hidden_out = jnp.concatenate(out_list, axis=1)
    keys_all = jnp.concatenate(key_list, axis=1)
    values_all = jnp.concatenate(value_list, axis=1)
    slot_hits = slot_ids[None, None, :] == positions[:, :, None]
    one_hot = slot_hits.astype(jnp.bfloat16)
    written = jnp.any(slot_hits, axis=1)[..., None]
    placed_keys = jnp.einsum(
        "rts,rtm->rsm",
        one_hot,
        keys_all.reshape(requests, token_count, local_width),
        preferred_element_type=jnp.float32,
    ).astype(jnp.bfloat16)
    placed_values = jnp.einsum(
        "rts,rtm->rsm",
        one_hot,
        values_all.reshape(requests, token_count, local_width),
        preferred_element_type=jnp.float32,
    ).astype(jnp.bfloat16)
    new_cache_keys = jnp.where(written, placed_keys, cache_keys)
    new_cache_values = jnp.where(written, placed_values, cache_values)
    return (hidden_out, new_cache_keys, new_cache_values)


def solution(mesh):
    placed = (
        P(None, None, "seq"),
        P(None, "seq", "mdl"),
        P(None, "seq", "mdl"),
        P(),
        P("seq", "mdl"),
        P("seq", "mdl"),
        P("seq", "mdl"),
        P("mdl", "seq"),
        P("seq", "mdl"),
        P("seq", "mdl"),
        P("mdl", "seq"),
    )
    return jax.shard_map(
        body,
        mesh=mesh,
        in_specs=placed,
        out_specs=(P(None, None, "seq"), P(None, "seq", "mdl"), P(None, "seq", "mdl")),
        check_vma=False,
    )
```

```python
import functools
import math

import jax
import jax.numpy as jnp
from jax import lax
from jax.experimental import pallas as pl
from jax.experimental.pallas import tpu as pltpu
from jax.sharding import PartitionSpec as P

D = 2048
HEADS = 16


EPS = 1e-05
THETA = 10000.0
NEGATIVE = -1e30


def rotate(vectors, placed_pos):
    head_size = vectors.shape[-1]
    half_dim = head_size // 2
    freqs = THETA ** (-jnp.arange(half_dim, dtype=jnp.float32) * 2.0 / head_size)
    angles = placed_pos.astype(jnp.float32)[..., None, None] * freqs
    cosine = jnp.cos(angles)
    sine = jnp.sin(angles)
    first_half = vectors[..., :half_dim]
    second_half = vectors[..., half_dim:]
    return jnp.concatenate(
        [first_half * cosine - second_half * sine, second_half * cosine + first_half * sine],
        axis=-1,
    )


def normalize(widened, row_sums, square_sums):
    row_mean = row_sums / D
    second_moment = square_sums / D
    inverse = 1.0 / jnp.sqrt(second_moment - row_mean * row_mean + EPS)
    return ((widened - row_mean[..., None]) * inverse[..., None]).astype(jnp.bfloat16)


def body_plain(
    hidden_in,
    cache_keys,
    cache_values,
    lengths,
    query_weight,
    key_weight,
    value_weight,
    out_weight,
    gate_weight,
    up_weight,
    down_weight,
):
    requests, token_count, narrow_width = hidden_in.shape
    slot_count = cache_keys.shape[1]
    local_width = cache_keys.shape[2]
    head_size = D // HEADS
    local_heads = local_width // head_size
    score_scale = 1.0 / math.sqrt(head_size)
    shard_index = lax.axis_index("seq")
    slot_ids = shard_index * slot_count + jnp.arange(slot_count, dtype=jnp.int32)
    live_slots = slot_ids[None, :] < lengths[:, None]
    old_keys = cache_keys.reshape(requests, slot_count, local_heads, head_size)
    old_values = cache_values.reshape(requests, slot_count, local_heads, head_size).astype(
        jnp.float32
    )
    positions = lengths[:, None] + jnp.arange(token_count, dtype=jnp.int32)[None, :]
    out_list = []
    key_list = []
    value_list = []
    for token_step in range(1):
        row_block = hidden_in
        block_rows = row_block.shape[1]
        widened = row_block.astype(jnp.float32)
        row_sums, square_sums = lax.psum(
            (jnp.sum(widened, axis=-1), jnp.sum(widened * widened, axis=-1)), "seq"
        )
        normed = normalize(widened, row_sums, square_sums)
        query_part = jnp.einsum(
            "rnc,cm->rnm", normed, query_weight, preferred_element_type=jnp.float32
        )
        key_part = jnp.einsum("rnc,cm->rnm", normed, key_weight, preferred_element_type=jnp.float32)
        value_part = jnp.einsum(
            "rnc,cm->rnm", normed, value_weight, preferred_element_type=jnp.float32
        )
        queries, keys_full, values_full = lax.psum((query_part, key_part, value_part), "seq")
        placed_pos = positions[:, token_step : token_step + block_rows]
        queries = rotate(
            queries.reshape(requests, block_rows, local_heads, head_size), placed_pos
        ).astype(jnp.bfloat16)
        new_key = rotate(
            keys_full.reshape(requests, block_rows, local_heads, head_size), placed_pos
        ).astype(jnp.bfloat16)
        new_value = values_full.reshape(requests, block_rows, local_heads, head_size).astype(
            jnp.bfloat16
        )
        keys_new = jnp.concatenate(key_list + [new_key], axis=1)
        values_new = jnp.concatenate(value_list + [new_value], axis=1)
        old_scores = (
            jnp.einsum("rnhd,rjhd->rnhj", queries, old_keys, preferred_element_type=jnp.float32)
            * score_scale
        )
        old_scores = jnp.where(live_slots[:, None, None, :], old_scores, NEGATIVE)
        top_old = jnp.max(old_scores, axis=-1)
        weights_old = jnp.where(
            live_slots[:, None, None, :], jnp.exp(old_scores - top_old[..., None]), 0.0
        )
        total_old = jnp.sum(weights_old, axis=-1)
        summed_old = jnp.einsum(
            "rnhj,rjhd->rnhd", weights_old, old_values, precision=lax.Precision.HIGHEST
        )
        top_cache = lax.pmax(top_old, "seq")
        factor_old = jnp.exp(top_old - top_cache)
        total_cache, summed_cache = lax.psum(
            (total_old * factor_old, summed_old * factor_old[..., None]), "seq"
        )
        new_scores = (
            jnp.einsum("rnhd,rshd->rnhs", queries, keys_new, preferred_element_type=jnp.float32)
            * score_scale
        )
        key_index = jnp.arange(keys_new.shape[1], dtype=jnp.int32)
        query_index = token_step + jnp.arange(block_rows, dtype=jnp.int32)
        allowed = key_index[None, :] <= query_index[:, None]
        new_scores = jnp.where(allowed[None, :, None, :], new_scores, NEGATIVE)
        top_new = jnp.max(new_scores, axis=-1)
        weights_new = jnp.exp(new_scores - top_new[..., None])
        total_new = jnp.sum(weights_new, axis=-1)
        summed_new = jnp.einsum(
            "rnhs,rshd->rnhd",
            weights_new,
            values_new.astype(jnp.float32),
            precision=lax.Precision.HIGHEST,
        )
        top_score = jnp.maximum(top_cache, top_new)
        factor_cache = jnp.exp(top_cache - top_score)
        factor_new = jnp.exp(top_new - top_score)
        running = total_cache * factor_cache + total_new * factor_new
        combined = summed_cache * factor_cache[..., None] + summed_new * factor_new[..., None]
        attended = (
            (combined / running[..., None])
            .astype(jnp.bfloat16)
            .reshape(requests, block_rows, local_width)
        )
        attn_part = jnp.einsum(
            "rnm,mc->rnc", attended, out_weight, preferred_element_type=jnp.float32
        )
        mixed = widened + lax.psum(attn_part, "mdl")
        sums_mixed, squares_mixed = lax.psum(
            (jnp.sum(mixed, axis=-1), jnp.sum(mixed * mixed, axis=-1)), "seq"
        )
        normed2 = normalize(mixed, sums_mixed, squares_mixed)
        gate_part = jnp.einsum(
            "rnc,cf->rnf", normed2, gate_weight, preferred_element_type=jnp.float32
        )
        up_part = jnp.einsum("rnc,cf->rnf", normed2, up_weight, preferred_element_type=jnp.float32)
        gate_full, up_full = lax.psum((gate_part, up_part), "seq")
        act_full = (jax.nn.silu(gate_full) * up_full).astype(jnp.bfloat16)
        down_part = jnp.einsum(
            "rnf,fc->rnc", act_full, down_weight, preferred_element_type=jnp.float32
        )
        block_out = (mixed + lax.psum(down_part, "mdl")).astype(jnp.bfloat16)
        block_out, new_key, new_value = (block_out, new_key, new_value)
        out_list.append(block_out)
        key_list.append(new_key)
        value_list.append(new_value)
    hidden_out = jnp.concatenate(out_list, axis=1)
    keys_all = jnp.concatenate(key_list, axis=1)
    values_all = jnp.concatenate(value_list, axis=1)
    slot_hits = slot_ids[None, None, :] == positions[:, :, None]
    one_hot = slot_hits.astype(jnp.bfloat16)
    written = jnp.any(slot_hits, axis=1)[..., None]
    placed_keys = jnp.einsum(
        "rts,rtm->rsm",
        one_hot,
        keys_all.reshape(requests, token_count, local_width),
        preferred_element_type=jnp.float32,
    ).astype(jnp.bfloat16)
    placed_values = jnp.einsum(
        "rts,rtm->rsm",
        one_hot,
        values_all.reshape(requests, token_count, local_width),
        preferred_element_type=jnp.float32,
    ).astype(jnp.bfloat16)
    new_cache_keys = jnp.where(written, placed_keys, cache_keys)
    new_cache_values = jnp.where(written, placed_values, cache_values)
    return (hidden_out, new_cache_keys, new_cache_values)


PLANE = 4
MESH = pl.DeviceIdType.MESH
F32 = jnp.float32
BF16 = jnp.bfloat16


def plane_peer(me, j):
    p = me % PLANE
    x, y = p % 2, p // 2
    if j % 2:
        x = 1 - x
    if j // 2:
        y = 1 - y
    return (me // PLANE) * PLANE + y * 2 + x


def depth_peer(me, k, depth):
    return ((me // PLANE + k) % depth) * PLANE + me % PLANE


def remote(src, dst, send, recv, device):
    copy = pltpu.make_async_remote_copy(
        src_ref=src, dst_ref=dst, send_sem=send, recv_sem=recv, device_id=device, device_id_type=MESH
    )
    copy.start()
    return copy


def wait_all(copies):
    for copy in copies:
        copy.wait()


def enter(n, me, partner=None):
    barrier = pltpu.get_barrier_semaphore()
    for k in range(1, n):
        pl.semaphore_signal(
            barrier, inc=1, device_id={"seq": (me + k) % n}, device_id_type=MESH
        )
    if partner is not None:
        pl.semaphore_signal(barrier, inc=1, device_id={"mdl": partner}, device_id_type=MESH)
    pl.semaphore_wait(barrier, n - 1 + (partner is not None))


def share_small(n, me, slots, send, recv):
    wait_all(
        [
            remote(
                slots.at[me], slots.at[me], send.at[k - 1], recv.at[k - 1], {"seq": (me + k) % n}
            )
            for k in range(1, n)
        ]
    )


def scatter_sum(n, me, part, got_plane, half, got_depth, sems):
    depth = n // PLANE
    z, p = me // PLANE, me % PLANE
    copies = []
    for j in range(1, PLANE):
        peer = plane_peer(me, j)
        copies.append(
            remote(
                part.at[:, peer % PLANE],
                got_plane.at[j - 1],
                sems[0].at[j - 1],
                sems[1].at[j - 1],
                {"seq": peer},
            )
        )
    wait_all(copies)
    for d in range(depth):
        total = part[d, p].astype(F32)
        for j in range(PLANE - 1):
            total = total + got_plane[j, d].astype(F32)
        half[d] = total.astype(half.dtype)
    copies = []
    for k in range(1, depth):
        peer = depth_peer(me, k, depth)
        copies.append(
            remote(
                half.at[peer // PLANE],
                got_depth.at[k - 1],
                sems[2].at[k - 1],
                sems[3].at[k - 1],
                {"seq": peer},
            )
        )
    wait_all(copies)
    total = half[z].astype(F32)
    for k in range(depth - 1):
        total = total + got_depth[k].astype(F32)
    return total


def gather_rows(n, me, whole, sems):
    depth = n // PLANE
    z, p = me // PLANE, me % PLANE
    wait_all(
        [
            remote(
                whole.at[z, p],
                whole.at[z, p],
                sems[0].at[k - 1],
                sems[1].at[k - 1],
                {"seq": depth_peer(me, k, depth)},
            )
            for k in range(1, depth)
        ]
    )
    wait_all(
        [
            remote(
                whole.at[:, p],
                whole.at[:, p],
                sems[2].at[j - 1],
                sems[3].at[j - 1],
                {"seq": plane_peer(me, j)},
            )
            for j in range(1, PLANE)
        ]
    )


def row_stats(n, me, widened, slots, send, recv):
    rows = widened.shape[0]
    lanes = lax.broadcasted_iota(jnp.int32, (rows, 128), 1)
    first = jnp.sum(widened, axis=-1, keepdims=True)
    second = jnp.sum(widened * widened, axis=-1, keepdims=True)
    packed = jnp.where(lanes == 0, first, jnp.where(lanes == 1, second, 0.0))
    slots[me] = packed.T[0:8]
    share_small(n, me, slots, send, recv)
    total = slots[0]
    for i in range(1, n):
        total = total + slots[i]
    back = jnp.concatenate([total, jnp.zeros((120, rows), F32)], axis=0).T
    return back[:, 0:1], back[:, 1:2]


def normalize_rows(widened, first, second):
    mean = first / D
    inverse = 1.0 / jnp.sqrt(second / D - mean * mean + EPS)
    return ((widened - mean) * inverse).astype(BF16)


def project_kernel(
    n, x_ref, wq, wk, wv, cos_ref, sin_ref, whole, own, part, got_plane, half, got_depth, slots, *sems
):
    me = lax.axis_index("seq")
    enter(n, me)
    widened = x_ref[...].astype(F32)
    normed = normalize_rows(widened, *row_stats(n, me, widened, slots, sems[0], sems[1]))
    width = wq.shape[1]
    shape = part.shape[:3] + (width,)
    for i, w in enumerate((wq, wk, wv)):
        made = jnp.dot(normed, w[...], preferred_element_type=F32)
        part[:, :, :, i * width : (i + 1) * width] = made.reshape(shape)
    sums = scatter_sum(n, me, part, got_plane, half, got_depth, sems[2:6])
    cosine, sine = cos_ref[me], sin_ref[me]
    z, p = me // PLANE, me % PLANE
    for c in range(3 * width // 128):
        piece = sums[:, c * 128 : (c + 1) * 128]
        if c < 2 * width // 128:
            piece = piece * cosine + pltpu.roll(piece, 64, 1) * sine
        whole[z, p, :, c * 128 : (c + 1) * 128] = piece.astype(BF16)
    own[...] = whole[z, p]
    gather_rows(n, me, whole, sems[6:10])


def attend_kernel(
    n,
    scale,
    stat_ref,
    acc_ref,
    own_ref,
    x_ref,
    w_ref,
    mixed_ref,
    normed_ref,
    part,
    got_plane,
    half,
    got_depth,
    tops,
    slots,
    back_ref,
    whole,
    mine,
    other,
    *sems,
):
    me = lax.axis_index("seq")
    partner = 1 - lax.axis_index("mdl")
    enter(n, me, partner)
    rows = stat_ref.shape[0]
    width = acc_ref.shape[1]
    heads = width // 128
    stat = stat_ref[...]
    tops[me] = stat.T[0:8]
    share_small(n, me, tops, sems[0], sems[1])
    top = tops[0]
    for i in range(1, n):
        top = jnp.maximum(top, tops[i])
    back = jnp.concatenate([top, jnp.zeros((120, rows), F32)], axis=0).T
    back_ref[...] = back.reshape(back_ref.shape)
    factor = jnp.exp(stat - back)
    shape = part.shape[:3] + (128,)
    for h in range(heads):
        cols = slice(h * 128, (h + 1) * 128)
        part[:, :, :, cols] = (acc_ref[:, cols] * factor[:, h : h + 1]).reshape(shape)
    lanes = lax.broadcasted_iota(jnp.int32, (rows, 128), 1)
    totals = jnp.where(lanes < heads, pltpu.roll(stat, 128 - heads, 1) * factor, 0.0)
    part[:, :, :, width : width + 128] = totals.reshape(shape)
    sums = scatter_sum(n, me, part, got_plane, half, got_depth, sems[2:6])
    z, p = me // PLANE, me % PLANE
    top_own = back_ref[me]
    token = lax.broadcasted_iota(jnp.int32, (8, 8), 0)
    key = lax.broadcasted_iota(jnp.int32, (8, 8), 1)
    allowed = (token // 4 == key // 4) & (key <= token)
    for h in range(heads):
        cols = slice(h * 128, (h + 1) * 128)
        query = own_ref[:, h * 128 : (h + 1) * 128]
        keys = own_ref[:, width + h * 128 : width + (h + 1) * 128]
        values = own_ref[:, 2 * width + h * 128 : 2 * width + (h + 1) * 128]
        scores = (
            lax.dot_general(query, keys, (((1,), (1,)), ((), ())), preferred_element_type=F32)
            * scale
        )
        scores = jnp.where(allowed, scores, NEGATIVE)
        top_cache = top_own[:, h : h + 1]
        top_all = jnp.maximum(top_cache, jnp.max(scores, axis=-1, keepdims=True))
        weights = jnp.where(allowed, jnp.exp(scores - top_all), 0.0)
        kept = jnp.exp(top_cache - top_all)
        running = sums[:, width + h : width + h + 1] * kept + jnp.sum(
            weights, axis=-1, keepdims=True
        )
        summed = sums[:, cols] * kept + jnp.dot(
            weights,
            values.astype(F32),
            precision=lax.Precision.HIGHEST,
            preferred_element_type=F32,
        )
        whole[z, p, :, cols] = (summed / running).astype(BF16)
    gather_rows(n, me, whole, sems[6:10])
    attended = whole[...].astype(F32).reshape(rows, width).astype(BF16)
    made = jnp.dot(attended, w_ref[...], preferred_element_type=F32)
    mine[...] = made
    remote(mine, other, sems[12].at[0], sems[13].at[0], {"mdl": partner}).wait()
    mixed = x_ref[...].astype(F32) + (made + other[...])
    mixed_ref[...] = mixed
    normed_ref[...] = normalize_rows(
        mixed, *row_stats(n, me, mixed, slots, sems[10], sems[11])
    )


def feed_kernel(
    n,
    normed_ref,
    mixed_ref,
    wg,
    wu,
    wd,
    out_ref,
    part,
    got_plane,
    half,
    got_depth,
    whole,
    mine,
    other,
    *sems,
):
    me = lax.axis_index("seq")
    partner = 1 - lax.axis_index("mdl")
    enter(n, me, partner)
    rows = normed_ref.shape[0]
    width = wg.shape[1]
    tile = 1024
    normed = normed_ref[...]
    shape = part.shape[:3] + (tile,)
    for i, w in enumerate((wg, wu)):
        for t in range(0, width, tile):
            made = jnp.dot(normed, w[:, t : t + tile], preferred_element_type=F32)
            part[:, :, :, i * width + t : i * width + t + tile] = made.reshape(shape).astype(
                part.dtype
            )
    sums = scatter_sum(n, me, part, got_plane, half, got_depth, sems[0:4])
    z, p = me // PLANE, me % PLANE
    gate, up = sums[:, :width], sums[:, width:]
    whole[z, p] = (gate / (1.0 + jnp.exp(-gate)) * up).astype(BF16)
    gather_rows(n, me, whole, sems[4:8])
    total = jnp.zeros((rows, out_ref.shape[1]), F32)
    for t in range(0, width, tile):
        act = whole[:, :, :, t : t + tile].astype(F32).reshape(rows, tile).astype(BF16)
        total = total + jnp.dot(act, wd[t : t + tile], preferred_element_type=F32)
    mine[...] = total
    remote(mine, other, sems[8].at[0], sems[9].at[0], {"mdl": partner}).wait()
    out_ref[...] = mixed_ref[...] + (total + other[...])


def pair(count):
    return [pltpu.SemaphoreType.DMA((count,))] * 2


def call(kernel, identity, outs, scratch, *operands):
    vmem = pl.BlockSpec(memory_space=pltpu.VMEM)
    return pl.pallas_call(
        kernel,
        out_shape=outs,
        in_specs=[vmem] * len(operands),
        out_specs=[vmem] * len(outs),
        scratch_shapes=scratch,
        compiler_params=pltpu.CompilerParams(
            collective_id=identity, has_side_effects=True, vmem_limit_bytes=48 * 2**20
        ),
    )(*operands)


def sum_scratch(depth, width, dtype):
    return [
        pltpu.VMEM((depth, PLANE, 8, width), dtype),
        pltpu.VMEM((PLANE - 1, depth, 8, width), dtype),
        pltpu.VMEM((depth, 8, width), dtype),
        pltpu.VMEM((depth - 1, 8, width), dtype),
    ]


def body_kernels(
    n,
    hidden_in,
    cache_keys,
    cache_values,
    lengths,
    query_weight,
    key_weight,
    value_weight,
    out_weight,
    gate_weight,
    up_weight,
    down_weight,
):
    requests, token_count, narrow = hidden_in.shape
    rows = requests * token_count
    depth = n // PLANE
    slot_count, local_width = cache_keys.shape[1:]
    head_size = D // HEADS
    local_heads = local_width // head_size
    score_scale = 1.0 / math.sqrt(head_size)
    shard_index = lax.axis_index("seq")
    slot_ids = shard_index * slot_count + jnp.arange(slot_count, dtype=jnp.int32)
    live_slots = slot_ids[None, :] < lengths[:, None]
    positions = lengths[:, None] + jnp.arange(token_count, dtype=jnp.int32)[None, :]
    half_dim = head_size // 2
    freqs = THETA ** (-jnp.arange(half_dim, dtype=F32) * 2.0 / head_size)
    angles = positions.reshape(rows, 1).astype(F32) * freqs
    cosine, sine = jnp.cos(angles), jnp.sin(angles)
    cosine = jnp.concatenate([cosine, cosine], axis=-1).reshape(n, 8, head_size)
    sine = jnp.concatenate([-sine, sine], axis=-1).reshape(n, 8, head_size)
    x = hidden_in.reshape(rows, narrow)
    struct = jax.ShapeDtypeStruct
    whole, own = call(
        functools.partial(project_kernel, n),
        1,
        [struct((depth, PLANE, 8, 3 * local_width), BF16), struct((8, 3 * local_width), BF16)],
        sum_scratch(depth, 3 * local_width, F32)
        + [pltpu.VMEM((n, 8, 128), F32)]
        + pair(n - 1)
        + pair(PLANE - 1)
        + pair(depth - 1)
        + pair(depth - 1)
        + pair(PLANE - 1),
        x,
        query_weight,
        key_weight,
        value_weight,
        cosine,
        sine,
    )
    whole = whole.reshape(requests, token_count, 3 * local_width)
    keys_all = whole[..., local_width : 2 * local_width]
    values_all = whole[..., 2 * local_width :]
    queries = whole[..., :local_width].reshape(requests, token_count, local_heads, head_size)
    old_keys = cache_keys.reshape(requests, slot_count, local_heads, head_size)
    old_values = cache_values.reshape(requests, slot_count, local_heads, head_size).astype(F32)
    old_scores = (
        jnp.einsum("rnhd,rjhd->rnhj", queries, old_keys, preferred_element_type=F32) * score_scale
    )
    old_scores = jnp.where(live_slots[:, None, None, :], old_scores, NEGATIVE)
    top_old = jnp.max(old_scores, axis=-1)
    weights_old = jnp.where(
        live_slots[:, None, None, :], jnp.exp(old_scores - top_old[..., None]), 0.0
    )
    total_old = jnp.sum(weights_old, axis=-1)
    summed_old = jnp.einsum(
        "rnhj,rjhd->rnhd", weights_old, old_values, precision=lax.Precision.HIGHEST
    )
    stat = jnp.concatenate(
        [
            top_old.reshape(rows, local_heads),
            total_old.reshape(rows, local_heads),
            jnp.zeros((rows, 128 - 2 * local_heads), F32),
        ],
        axis=-1,
    )
    mixed, normed2 = call(
        functools.partial(attend_kernel, n, score_scale),
        2,
        [struct((rows, narrow), F32), struct((rows, narrow), BF16)],
        sum_scratch(depth, local_width + 128, F32)
        + [
            pltpu.VMEM((n, 8, 128), F32),
            pltpu.VMEM((n, 8, 128), F32),
            pltpu.VMEM((n, 8, 128), F32),
            pltpu.VMEM((depth, PLANE, 8, local_width), BF16),
            pltpu.VMEM((rows, narrow), F32),
            pltpu.VMEM((rows, narrow), F32),
        ]
        + pair(n - 1)
        + pair(PLANE - 1)
        + pair(depth - 1)
        + pair(depth - 1)
        + pair(PLANE - 1)
        + pair(n - 1)
        + pair(1),
        stat,
        summed_old.reshape(rows, local_width),
        own,
        x,
        out_weight,
    )
    ff = gate_weight.shape[1]
    (block_out,) = call(
        functools.partial(feed_kernel, n),
        3,
        [struct((rows, narrow), F32)],
        sum_scratch(depth, 2 * ff, BF16)
        + [
            pltpu.VMEM((depth, PLANE, 8, ff), BF16),
            pltpu.VMEM((rows, narrow), F32),
            pltpu.VMEM((rows, narrow), F32),
        ]
        + pair(PLANE - 1)
        + pair(depth - 1)
        + pair(depth - 1)
        + pair(PLANE - 1)
        + pair(1),
        normed2,
        mixed,
        gate_weight,
        up_weight,
        down_weight,
    )
    hidden_out = block_out.astype(BF16).reshape(requests, token_count, narrow)
    new_keys, new_values = write_rows(
        slot_ids, positions, keys_all, values_all, cache_keys, cache_values
    )
    return hidden_out, new_keys, new_values


def write_rows(slot_ids, positions, keys_all, values_all, cache_keys, cache_values):
    slot_hits = slot_ids[None, None, :] == positions[:, :, None]
    one_hot = slot_hits.astype(BF16)
    written = jnp.any(slot_hits, axis=1)[..., None]
    placed = [
        jnp.einsum("rts,rtm->rsm", one_hot, rows, preferred_element_type=F32).astype(BF16)
        for rows in (keys_all, values_all)
    ]
    return (
        jnp.where(written, placed[0], cache_keys),
        jnp.where(written, placed[1], cache_values),
    )


def body(n, model_shards, hidden_in, cache_keys, *rest):
    rows = hidden_in.shape[0] * hidden_in.shape[1]
    tiled = (
        n % PLANE == 0
        and rows == 128
        and rows // n == 8
        and hidden_in.shape[1] == 4
        and hidden_in.shape[2] == 128
        and model_shards == 2
    )
    if tiled:
        return body_kernels(n, hidden_in, cache_keys, *rest)
    return body_plain(hidden_in, cache_keys, *rest)


def solution(mesh):
    placed = (
        P(None, None, "seq"),
        P(None, "seq", "mdl"),
        P(None, "seq", "mdl"),
        P(),
        P("seq", "mdl"),
        P("seq", "mdl"),
        P("seq", "mdl"),
        P("mdl", "seq"),
        P("seq", "mdl"),
        P("seq", "mdl"),
        P("mdl", "seq"),
    )
    return jax.shard_map(
        functools.partial(body, mesh.shape["seq"], mesh.shape["mdl"]),
        mesh=mesh,
        in_specs=placed,
        out_specs=(P(None, None, "seq"), P(None, "seq", "mdl"), P(None, "seq", "mdl")),
        check_vma=False,
    )
```

```python
import functools
import math

import jax
import jax.numpy as jnp
from jax import lax
from jax.experimental import pallas as pl
from jax.experimental.pallas import tpu as pltpu
from jax.sharding import PartitionSpec as P

D = 2048
HEADS = 16


EPS = 1e-05
THETA = 10000.0
NEGATIVE = -1e30


def rotate(vectors, placed_pos):
    head_size = vectors.shape[-1]
    half_dim = head_size // 2
    freqs = THETA ** (-jnp.arange(half_dim, dtype=jnp.float32) * 2.0 / head_size)
    angles = placed_pos.astype(jnp.float32)[..., None, None] * freqs
    cosine = jnp.cos(angles)
    sine = jnp.sin(angles)
    first_half = vectors[..., :half_dim]
    second_half = vectors[..., half_dim:]
    return jnp.concatenate(
        [first_half * cosine - second_half * sine, second_half * cosine + first_half * sine],
        axis=-1,
    )


def normalize(widened, row_sums, square_sums):
    row_mean = row_sums / D
    second_moment = square_sums / D
    inverse = 1.0 / jnp.sqrt(second_moment - row_mean * row_mean + EPS)
    return ((widened - row_mean[..., None]) * inverse[..., None]).astype(jnp.bfloat16)


def body_plain(
    hidden_in,
    cache_keys,
    cache_values,
    lengths,
    query_weight,
    key_weight,
    value_weight,
    out_weight,
    gate_weight,
    up_weight,
    down_weight,
):
    requests, token_count, narrow_width = hidden_in.shape
    slot_count = cache_keys.shape[1]
    local_width = cache_keys.shape[2]
    head_size = D // HEADS
    local_heads = local_width // head_size
    score_scale = 1.0 / math.sqrt(head_size)
    shard_index = lax.axis_index("seq")
    slot_ids = shard_index * slot_count + jnp.arange(slot_count, dtype=jnp.int32)
    live_slots = slot_ids[None, :] < lengths[:, None]
    old_keys = cache_keys.reshape(requests, slot_count, local_heads, head_size)
    old_values = cache_values.reshape(requests, slot_count, local_heads, head_size).astype(
        jnp.float32
    )
    positions = lengths[:, None] + jnp.arange(token_count, dtype=jnp.int32)[None, :]
    out_list = []
    key_list = []
    value_list = []
    for token_step in range(1):
        row_block = hidden_in
        block_rows = row_block.shape[1]
        widened = row_block.astype(jnp.float32)
        row_sums, square_sums = lax.psum(
            (jnp.sum(widened, axis=-1), jnp.sum(widened * widened, axis=-1)), "seq"
        )
        normed = normalize(widened, row_sums, square_sums)
        query_part = jnp.einsum(
            "rnc,cm->rnm", normed, query_weight, preferred_element_type=jnp.float32
        )
        key_part = jnp.einsum("rnc,cm->rnm", normed, key_weight, preferred_element_type=jnp.float32)
        value_part = jnp.einsum(
            "rnc,cm->rnm", normed, value_weight, preferred_element_type=jnp.float32
        )
        queries, keys_full, values_full = lax.psum((query_part, key_part, value_part), "seq")
        placed_pos = positions[:, token_step : token_step + block_rows]
        queries = rotate(
            queries.reshape(requests, block_rows, local_heads, head_size), placed_pos
        ).astype(jnp.bfloat16)
        new_key = rotate(
            keys_full.reshape(requests, block_rows, local_heads, head_size), placed_pos
        ).astype(jnp.bfloat16)
        new_value = values_full.reshape(requests, block_rows, local_heads, head_size).astype(
            jnp.bfloat16
        )
        keys_new = jnp.concatenate(key_list + [new_key], axis=1)
        values_new = jnp.concatenate(value_list + [new_value], axis=1)
        old_scores = (
            jnp.einsum("rnhd,rjhd->rnhj", queries, old_keys, preferred_element_type=jnp.float32)
            * score_scale
        )
        old_scores = jnp.where(live_slots[:, None, None, :], old_scores, NEGATIVE)
        top_old = jnp.max(old_scores, axis=-1)
        weights_old = jnp.where(
            live_slots[:, None, None, :], jnp.exp(old_scores - top_old[..., None]), 0.0
        )
        total_old = jnp.sum(weights_old, axis=-1)
        summed_old = jnp.einsum(
            "rnhj,rjhd->rnhd", weights_old, old_values, precision=lax.Precision.HIGHEST
        )
        top_cache = lax.pmax(top_old, "seq")
        factor_old = jnp.exp(top_old - top_cache)
        total_cache, summed_cache = lax.psum(
            (total_old * factor_old, summed_old * factor_old[..., None]), "seq"
        )
        new_scores = (
            jnp.einsum("rnhd,rshd->rnhs", queries, keys_new, preferred_element_type=jnp.float32)
            * score_scale
        )
        key_index = jnp.arange(keys_new.shape[1], dtype=jnp.int32)
        query_index = token_step + jnp.arange(block_rows, dtype=jnp.int32)
        allowed = key_index[None, :] <= query_index[:, None]
        new_scores = jnp.where(allowed[None, :, None, :], new_scores, NEGATIVE)
        top_new = jnp.max(new_scores, axis=-1)
        weights_new = jnp.exp(new_scores - top_new[..., None])
        total_new = jnp.sum(weights_new, axis=-1)
        summed_new = jnp.einsum(
            "rnhs,rshd->rnhd",
            weights_new,
            values_new.astype(jnp.float32),
            precision=lax.Precision.HIGHEST,
        )
        top_score = jnp.maximum(top_cache, top_new)
        factor_cache = jnp.exp(top_cache - top_score)
        factor_new = jnp.exp(top_new - top_score)
        running = total_cache * factor_cache + total_new * factor_new
        combined = summed_cache * factor_cache[..., None] + summed_new * factor_new[..., None]
        attended = (
            (combined / running[..., None])
            .astype(jnp.bfloat16)
            .reshape(requests, block_rows, local_width)
        )
        attn_part = jnp.einsum(
            "rnm,mc->rnc", attended, out_weight, preferred_element_type=jnp.float32
        )
        mixed = widened + lax.psum(attn_part, "mdl")
        sums_mixed, squares_mixed = lax.psum(
            (jnp.sum(mixed, axis=-1), jnp.sum(mixed * mixed, axis=-1)), "seq"
        )
        normed2 = normalize(mixed, sums_mixed, squares_mixed)
        gate_part = jnp.einsum(
            "rnc,cf->rnf", normed2, gate_weight, preferred_element_type=jnp.float32
        )
        up_part = jnp.einsum("rnc,cf->rnf", normed2, up_weight, preferred_element_type=jnp.float32)
        gate_full, up_full = lax.psum((gate_part, up_part), "seq")
        act_full = (jax.nn.silu(gate_full) * up_full).astype(jnp.bfloat16)
        down_part = jnp.einsum(
            "rnf,fc->rnc", act_full, down_weight, preferred_element_type=jnp.float32
        )
        block_out = (mixed + lax.psum(down_part, "mdl")).astype(jnp.bfloat16)
        block_out, new_key, new_value = (block_out, new_key, new_value)
        out_list.append(block_out)
        key_list.append(new_key)
        value_list.append(new_value)
    hidden_out = jnp.concatenate(out_list, axis=1)
    keys_all = jnp.concatenate(key_list, axis=1)
    values_all = jnp.concatenate(value_list, axis=1)
    slot_hits = slot_ids[None, None, :] == positions[:, :, None]
    one_hot = slot_hits.astype(jnp.bfloat16)
    written = jnp.any(slot_hits, axis=1)[..., None]
    placed_keys = jnp.einsum(
        "rts,rtm->rsm",
        one_hot,
        keys_all.reshape(requests, token_count, local_width),
        preferred_element_type=jnp.float32,
    ).astype(jnp.bfloat16)
    placed_values = jnp.einsum(
        "rts,rtm->rsm",
        one_hot,
        values_all.reshape(requests, token_count, local_width),
        preferred_element_type=jnp.float32,
    ).astype(jnp.bfloat16)
    new_cache_keys = jnp.where(written, placed_keys, cache_keys)
    new_cache_values = jnp.where(written, placed_values, cache_values)
    return (hidden_out, new_cache_keys, new_cache_values)


PLANE = 4
MESH = pl.DeviceIdType.MESH
F32 = jnp.float32
BF16 = jnp.bfloat16


def plane_peer(me, j):
    p = me % PLANE
    x, y = p % 2, p // 2
    if j % 2:
        x = 1 - x
    if j // 2:
        y = 1 - y
    return (me // PLANE) * PLANE + y * 2 + x


def depth_peer(me, k, depth):
    return ((me // PLANE + k) % depth) * PLANE + me % PLANE


def remote(src, dst, send, recv, device):
    copy = pltpu.make_async_remote_copy(
        src_ref=src, dst_ref=dst, send_sem=send, recv_sem=recv, device_id=device, device_id_type=MESH
    )
    copy.start()
    return copy


def wait_all(copies):
    for copy in copies:
        copy.wait()


def enter(n, me, partner=None):
    barrier = pltpu.get_barrier_semaphore()
    for k in range(1, n):
        pl.semaphore_signal(
            barrier, inc=1, device_id={"seq": (me + k) % n}, device_id_type=MESH
        )
    if partner is not None:
        pl.semaphore_signal(barrier, inc=1, device_id={"mdl": partner}, device_id_type=MESH)
    pl.semaphore_wait(barrier, n - 1 + (partner is not None))


def share_small(n, me, slots, send, recv):
    wait_all(
        [
            remote(
                slots.at[me], slots.at[me], send.at[k - 1], recv.at[k - 1], {"seq": (me + k) % n}
            )
            for k in range(1, n)
        ]
    )


def pipeline(
    n, me, fill, finish, consume, part, got_plane, half, got_depth, whole, *sems
):
    depth = n // PLANE
    chunks = part.shape[0]
    z, p = me // PLANE, me % PLANE
    flying = {}

    def send(kind, c, src, dst, pair_at, device):
        flying.setdefault((kind, c), []).append(
            remote(src, dst, sems[2 * kind].at[pair_at], sems[2 * kind + 1].at[pair_at], {"seq": device})
        )

    for c in range(chunks):
        fill(c)
        for j in range(1, PLANE):
            peer = plane_peer(me, j)
            send(
                0,
                c,
                part.at[c, :, peer % PLANE],
                got_plane.at[c, j - 1],
                c * (PLANE - 1) + j - 1,
                peer,
            )
    for step in range(chunks + 3):
        c = step
        if c < chunks:
            wait_all(flying[0, c])
            for d in range(depth):
                total = part[c, d, p].astype(F32)
                for j in range(PLANE - 1):
                    total = total + got_plane[c, j, d].astype(F32)
                half[c, d] = total.astype(half.dtype)
            for k in range(1, depth):
                peer = depth_peer(me, k, depth)
                send(
                    1,
                    c,
                    half.at[c, peer // PLANE],
                    got_depth.at[c, k - 1],
                    c * (depth - 1) + k - 1,
                    peer,
                )
        c = step - 1
        if 0 <= c < chunks:
            wait_all(flying[1, c])
            total = half[c, z].astype(F32)
            for k in range(depth - 1):
                total = total + got_depth[c, k].astype(F32)
            finish(c, total)
            for k in range(1, depth):
                mine = whole.at[c, z, p]
                send(
                    2, c, mine, mine, c * (depth - 1) + k - 1, depth_peer(me, k, depth)
                )
        c = step - 2
        if 0 <= c < chunks:
            wait_all(flying[2, c])
            for j in range(1, PLANE):
                mine = whole.at[c, :, p]
                send(3, c, mine, mine, c * (PLANE - 1) + j - 1, plane_peer(me, j))
        c = step - 3
        if 0 <= c < chunks:
            wait_all(flying[3, c])
            consume(c)


def row_stats(n, me, widened, slots, send, recv):
    rows = widened.shape[0]
    lanes = lax.broadcasted_iota(jnp.int32, (rows, 128), 1)
    first = jnp.sum(widened, axis=-1, keepdims=True)
    second = jnp.sum(widened * widened, axis=-1, keepdims=True)
    packed = jnp.where(lanes == 0, first, jnp.where(lanes == 1, second, 0.0))
    slots[me] = packed.T[0:8]
    share_small(n, me, slots, send, recv)
    total = slots[0]
    for i in range(1, n):
        total = total + slots[i]
    back = jnp.concatenate([total, jnp.zeros((120, rows), F32)], axis=0).T
    return back[:, 0:1], back[:, 1:2]


def normalize_rows(widened, first, second):
    mean = first / D
    inverse = 1.0 / jnp.sqrt(second / D - mean * mean + EPS)
    return ((widened - mean) * inverse).astype(BF16)


def project_kernel(
    n, x_ref, wq, wk, wv, cos_ref, sin_ref, whole, own, held, arrived, slots, send, recv, *rest
):
    me = lax.axis_index("seq")
    loads = [
        pltpu.make_async_copy(w, held.at[i], arrived.at[i]) for i, w in enumerate((wq, wk, wv))
    ]
    for load in loads:
        load.start()
    enter(n, me)
    part, got_plane, half, got_depth = rest[:4]
    widened = x_ref[...].astype(F32)
    normed = normalize_rows(widened, *row_stats(n, me, widened, slots, send, recv))
    z, p = me // PLANE, me % PLANE

    def fill(c):
        loads[c].wait()
        made = jnp.dot(normed, held[c], preferred_element_type=F32)
        part[c] = made.reshape(part.shape[1:])

    def finish(c, sums):
        for i in range(sums.shape[1] // 128):
            piece = sums[:, i * 128 : (i + 1) * 128]
            if c < 2:
                piece = piece * cos_ref[me] + pltpu.roll(piece, 64, 1) * sin_ref[me]
            piece = piece.astype(BF16)
            whole[c, z, p, :, i * 128 : (i + 1) * 128] = piece
            own[c, :, i * 128 : (i + 1) * 128] = piece

    pipeline(
        n, me, fill, finish, lambda c: None, part, got_plane, half, got_depth, whole, *rest[4:]
    )


def cache_kernel(scale, len_ref, new_ref, k_ref, v_ref, stat_ref, acc_ref, ko_ref, vo_ref):
    step = pl.program_id(0)
    group, slots, width = k_ref.shape
    base = lax.axis_index("seq") * slots
    head_mask = lax.broadcasted_iota(jnp.int32, (8, width), 1) // 128 == (
        lax.broadcasted_iota(jnp.int32, (8, width), 0)
    )
    slot = base + lax.broadcasted_iota(jnp.int32, (32, slots), 1)
    sub = lax.broadcasted_iota(jnp.int32, (8, 128), 0)
    lane = lax.broadcasted_iota(jnp.int32, (8, 128), 1)
    for i in range(group):
        length = len_ref[step * group + i]
        at = (i % 2) * 4
        fresh = [new_ref[c, i // 2].astype(F32) for c in range(3)]
        keys, values = k_ref[i], v_ref[i]
        queries = jnp.concatenate(
            [jnp.where(head_mask, fresh[0][at + t : at + t + 1], 0.0) for t in range(4)], axis=0
        ).astype(BF16)
        scores = (
            lax.dot_general(queries, keys, (((1,), (1,)), ((), ())), preferred_element_type=F32)
            * scale
        )
        live = slot < length
        scores = jnp.where(live, scores, NEGATIVE)
        top = jnp.max(scores, axis=-1, keepdims=True)
        weights = jnp.where(live, jnp.exp(scores - top), 0.0)
        total = jnp.sum(weights, axis=-1, keepdims=True)
        coarse = weights.astype(BF16)
        fine = (weights - coarse.astype(F32)).astype(BF16)
        summed = jnp.dot(coarse, values, preferred_element_type=F32) + jnp.dot(
            fine, values, preferred_element_type=F32
        )
        for t in range(4):
            row = i * 4 + t
            part = slice(8 * t, 8 * t + 8)
            acc_ref[row : row + 1] = jnp.sum(
                jnp.where(head_mask, summed[part], 0.0), axis=0, keepdims=True
            )
            stat_ref[row : row + 1] = jnp.sum(
                jnp.where(
                    lane == sub, top[part], jnp.where(lane == sub + 8, total[part], 0.0)
                ),
                axis=0,
                keepdims=True,
            )
        ko_ref[i] = keys
        vo_ref[i] = values
        first = length - base

        @pl.when((first < slots) & (first > -4))
        def _():
            place = lax.broadcasted_iota(jnp.int32, (slots, width), 0)
            for rows, old, out in ((fresh[1], keys, ko_ref), (fresh[2], values, vo_ref)):
                held = old.astype(F32)
                for t in range(4):
                    held = jnp.where(place == first + t, rows[at + t : at + t + 1], held)
                out[i] = held.astype(BF16)


def attend_kernel(
    n,
    scale,
    stat_ref,
    acc_ref,
    own_ref,
    x_ref,
    w_ref,
    mixed_ref,
    normed_ref,
    tops,
    slots,
    back_ref,
    mine,
    other,
    top_send,
    top_recv,
    send,
    recv,
    swap_send,
    swap_recv,
    *rest,
):
    me = lax.axis_index("seq")
    partner = 1 - lax.axis_index("mdl")
    enter(n, me, partner)
    part, got_plane, half, got_depth, whole = rest[:5]
    rows = stat_ref.shape[0]
    heads = acc_ref.shape[1] // 128
    chunks = part.shape[0]
    each = heads // chunks
    stat = stat_ref[...]
    tops[me] = stat.T[0:8]
    share_small(n, me, tops, top_send, top_recv)
    top = tops[0]
    for i in range(1, n):
        top = jnp.maximum(top, tops[i])
    back = jnp.concatenate([top, jnp.zeros((120, rows), F32)], axis=0).T
    back_ref[...] = back.reshape(back_ref.shape)
    factor = jnp.exp(stat - back)
    shape = part.shape[1:4] + (128,)
    lanes = lax.broadcasted_iota(jnp.int32, (rows, 128), 1)
    totals = jnp.where(lanes < heads, pltpu.roll(stat, 128 - heads, 1) * factor, 0.0)
    z, p = me // PLANE, me % PLANE
    top_own = back_ref[me]
    token = lax.broadcasted_iota(jnp.int32, (8, 8), 0)
    key = lax.broadcasted_iota(jnp.int32, (8, 8), 1)
    allowed = (token // 4 == key // 4) & (key <= token)

    def fill(c):
        for i in range(each):
            h = c * each + i
            part[c, :, :, :, i * 128 : (i + 1) * 128] = (
                acc_ref[:, h * 128 : (h + 1) * 128] * factor[:, h : h + 1]
            ).reshape(shape)
        part[c, :, :, :, each * 128 :] = totals.reshape(shape)

    def finish(c, sums):
        for i in range(each):
            h = c * each + i
            cols = slice(h * 128, (h + 1) * 128)
            query, keys, values = own_ref[0, :, cols], own_ref[1, :, cols], own_ref[2, :, cols]
            scores = (
                lax.dot_general(query, keys, (((1,), (1,)), ((), ())), preferred_element_type=F32)
                * scale
            )
            scores = jnp.where(allowed, scores, NEGATIVE)
            top_cache = top_own[:, h : h + 1]
            top_all = jnp.maximum(top_cache, jnp.max(scores, axis=-1, keepdims=True))
            weights = jnp.where(allowed, jnp.exp(scores - top_all), 0.0)
            kept = jnp.exp(top_cache - top_all)
            at = each * 128 + h
            running = sums[:, at : at + 1] * kept + jnp.sum(weights, axis=-1, keepdims=True)
            summed = sums[:, i * 128 : (i + 1) * 128] * kept + jnp.dot(
                weights,
                values.astype(F32),
                precision=lax.Precision.HIGHEST,
                preferred_element_type=F32,
            )
            whole[c, z, p, :, i * 128 : (i + 1) * 128] = (summed / running).astype(BF16)

    def consume(c):
        width = each * 128
        attended = whole[c].astype(F32).reshape(rows, width).astype(BF16)
        made = jnp.dot(
            attended, w_ref[c * width : (c + 1) * width], preferred_element_type=F32
        )
        mine[...] = made if c == 0 else mine[...] + made

    pipeline(n, me, fill, finish, consume, *rest)
    remote(mine, other, swap_send.at[0], swap_recv.at[0], {"mdl": partner}).wait()
    mixed = x_ref[...].astype(F32) + (mine[...] + other[...])
    mixed_ref[...] = mixed
    normed_ref[...] = normalize_rows(mixed, *row_stats(n, me, mixed, slots, send, recv))


def feed_kernel(
    n,
    normed_ref,
    mixed_ref,
    wg,
    wu,
    wd,
    out_ref,
    mine,
    other,
    swap_send,
    swap_recv,
    *rest,
):
    me = lax.axis_index("seq")
    partner = 1 - lax.axis_index("mdl")
    enter(n, me, partner)
    part, got_plane, half, got_depth, whole = rest[:5]
    rows = normed_ref.shape[0]
    tile = whole.shape[-1]
    normed = normed_ref[...]
    shape = part.shape[1:4] + (tile,)
    z, p = me // PLANE, me % PLANE

    def fill(c):
        for i, w in enumerate((wg, wu)):
            made = jnp.dot(
                normed, w[:, c * tile : (c + 1) * tile], preferred_element_type=F32
            )
            part[c, :, :, :, i * tile : (i + 1) * tile] = made.reshape(shape).astype(part.dtype)

    def finish(c, sums):
        gate, up = sums[:, :tile], sums[:, tile:]
        whole[c, z, p] = (gate / (1.0 + jnp.exp(-gate)) * up).astype(BF16)

    def consume(c):
        act = whole[c].astype(F32).reshape(rows, tile).astype(BF16)
        made = jnp.dot(act, wd[c * tile : (c + 1) * tile], preferred_element_type=F32)
        mine[...] = made if c == 0 else mine[...] + made

    pipeline(n, me, fill, finish, consume, *rest)
    remote(mine, other, swap_send.at[0], swap_recv.at[0], {"mdl": partner}).wait()
    out_ref[...] = (mixed_ref[...] + (mine[...] + other[...])).astype(BF16)


def pair(count):
    return [pltpu.SemaphoreType.DMA((count,))] * 2


def call(kernel, identity, outs, scratch, *operands, far=()):
    vmem = pl.BlockSpec(memory_space=pltpu.VMEM)
    return pl.pallas_call(
        kernel,
        out_shape=outs,
        in_specs=[
            pl.BlockSpec(memory_space=pl.ANY) if i in far else vmem for i in range(len(operands))
        ],
        out_specs=[vmem] * len(outs),
        scratch_shapes=scratch,
        compiler_params=pltpu.CompilerParams(
            collective_id=identity, has_side_effects=True, vmem_limit_bytes=48 * 2**20
        ),
    )(*operands)


def sum_scratch(chunks, depth, width, dtype):
    return [
        pltpu.VMEM((chunks, depth, PLANE, 8, width), dtype),
        pltpu.VMEM((chunks, PLANE - 1, depth, 8, width), dtype),
        pltpu.VMEM((chunks, depth, 8, width), dtype),
        pltpu.VMEM((chunks, depth - 1, 8, width), dtype),
    ]


def pipe_sems(chunks, depth):
    plane, line = pair(chunks * (PLANE - 1)), pair(chunks * (depth - 1))
    return plane + line + line + plane


def body_kernels(
    n,
    hidden_in,
    cache_keys,
    cache_values,
    lengths,
    query_weight,
    key_weight,
    value_weight,
    out_weight,
    gate_weight,
    up_weight,
    down_weight,
):
    requests, token_count, narrow = hidden_in.shape
    rows = requests * token_count
    depth = n // PLANE
    slot_count, local_width = cache_keys.shape[1:]
    head_size = D // HEADS
    score_scale = 1.0 / math.sqrt(head_size)
    positions = lengths[:, None] + jnp.arange(token_count, dtype=jnp.int32)[None, :]
    half_dim = head_size // 2
    freqs = THETA ** (-jnp.arange(half_dim, dtype=F32) * 2.0 / head_size)
    angles = positions.reshape(rows, 1).astype(F32) * freqs
    cosine, sine = jnp.cos(angles), jnp.sin(angles)
    cosine = jnp.concatenate([cosine, cosine], axis=-1).reshape(n, 8, head_size)
    sine = jnp.concatenate([-sine, sine], axis=-1).reshape(n, 8, head_size)
    x = hidden_in.reshape(rows, narrow)
    struct = jax.ShapeDtypeStruct
    whole, own = call(
        functools.partial(project_kernel, n),
        1,
        [struct((3, depth, PLANE, 8, local_width), BF16), struct((3, 8, local_width), BF16)],
        [
            pltpu.VMEM((3, narrow, local_width), BF16),
            pltpu.SemaphoreType.DMA((3,)),
            pltpu.VMEM((n, 8, 128), F32),
        ]
        + pair(n - 1)
        + sum_scratch(3, depth, local_width, F32)
        + pipe_sems(3, depth),
        x,
        query_weight,
        key_weight,
        value_weight,
        cosine,
        sine,
        far=(1, 2, 3),
    )
    group = 4
    block = pl.BlockSpec((group, slot_count, local_width), lambda g: (g, 0, 0))
    stat, acc, new_keys, new_values = pl.pallas_call(
        functools.partial(cache_kernel, score_scale),
        grid=(requests // group,),
        out_shape=[
            struct((rows, 128), F32),
            struct((rows, local_width), F32),
            struct(cache_keys.shape, BF16),
            struct(cache_values.shape, BF16),
        ],
        in_specs=[
            pl.BlockSpec(memory_space=pltpu.SMEM),
            pl.BlockSpec((3, group // 2, 8, local_width), lambda g: (0, g, 0, 0)),
            block,
            block,
        ],
        out_specs=[
            pl.BlockSpec((group * 4, 128), lambda g: (g, 0)),
            pl.BlockSpec((group * 4, local_width), lambda g: (g, 0)),
            block,
            block,
        ],
    )(lengths, whole.reshape(3, n, 8, local_width), cache_keys, cache_values)
    mixed, normed2 = call(
        functools.partial(attend_kernel, n, score_scale),
        2,
        [struct((rows, narrow), F32), struct((rows, narrow), BF16)],
        [
            pltpu.VMEM((n, 8, 128), F32),
            pltpu.VMEM((n, 8, 128), F32),
            pltpu.VMEM((n, 8, 128), F32),
            pltpu.VMEM((rows, narrow), F32),
            pltpu.VMEM((rows, narrow), F32),
        ]
        + pair(n - 1)
        + pair(n - 1)
        + pair(1)
        + sum_scratch(2, depth, local_width // 2 + 128, F32)
        + [pltpu.VMEM((2, depth, PLANE, 8, local_width // 2), BF16)]
        + pipe_sems(2, depth),
        stat,
        acc,
        own,
        x,
        out_weight,
    )
    ff = gate_weight.shape[1]
    chunks = ff // 1024
    (block_out,) = call(
        functools.partial(feed_kernel, n),
        3,
        [struct((rows, narrow), BF16)],
        [pltpu.VMEM((rows, narrow), F32), pltpu.VMEM((rows, narrow), F32)]
        + pair(1)
        + sum_scratch(chunks, depth, 2 * ff // chunks, BF16)
        + [pltpu.VMEM((chunks, depth, PLANE, 8, ff // chunks), BF16)]
        + pipe_sems(chunks, depth),
        normed2,
        mixed,
        gate_weight,
        up_weight,
        down_weight,
    )
    return block_out.reshape(requests, token_count, narrow), new_keys, new_values


def body(n, model_shards, hidden_in, cache_keys, *rest):
    rows = hidden_in.shape[0] * hidden_in.shape[1]
    tiled = (
        n % PLANE == 0
        and rows == 128
        and rows // n == 8
        and hidden_in.shape[1] == 4
        and hidden_in.shape[2] == 128
        and cache_keys.shape[2] == 1024
        and model_shards == 2
    )
    if tiled:
        return body_kernels(n, hidden_in, cache_keys, *rest)
    return body_plain(hidden_in, cache_keys, *rest)


def solution(mesh):
    placed = (
        P(None, None, "seq"),
        P(None, "seq", "mdl"),
        P(None, "seq", "mdl"),
        P(),
        P("seq", "mdl"),
        P("seq", "mdl"),
        P("seq", "mdl"),
        P("mdl", "seq"),
        P("seq", "mdl"),
        P("seq", "mdl"),
        P("mdl", "seq"),
    )
    return jax.shard_map(
        functools.partial(body, mesh.shape["seq"], mesh.shape["mdl"]),
        mesh=mesh,
        in_specs=placed,
        out_specs=(P(None, None, "seq"), P(None, "seq", "mdl"), P(None, "seq", "mdl")),
        check_vma=False,
    )
```

```python
import functools
import math

import jax
import jax.numpy as jnp
from jax import lax
from jax.experimental import pallas as pl
from jax.experimental.pallas import tpu as pltpu
from jax.sharding import PartitionSpec as P

D = 2048
HEADS = 16


EPS = 1e-05
THETA = 10000.0
NEGATIVE = -1e30


def rotate(vectors, placed_pos):
    head_size = vectors.shape[-1]
    half_dim = head_size // 2
    freqs = THETA ** (-jnp.arange(half_dim, dtype=jnp.float32) * 2.0 / head_size)
    angles = placed_pos.astype(jnp.float32)[..., None, None] * freqs
    cosine = jnp.cos(angles)
    sine = jnp.sin(angles)
    first_half = vectors[..., :half_dim]
    second_half = vectors[..., half_dim:]
    return jnp.concatenate(
        [first_half * cosine - second_half * sine, second_half * cosine + first_half * sine],
        axis=-1,
    )


def normalize(widened, row_sums, square_sums):
    row_mean = row_sums / D
    second_moment = square_sums / D
    inverse = 1.0 / jnp.sqrt(second_moment - row_mean * row_mean + EPS)
    return ((widened - row_mean[..., None]) * inverse[..., None]).astype(jnp.bfloat16)


def body_plain(
    hidden_in,
    cache_keys,
    cache_values,
    lengths,
    query_weight,
    key_weight,
    value_weight,
    out_weight,
    gate_weight,
    up_weight,
    down_weight,
):
    requests, token_count, narrow_width = hidden_in.shape
    slot_count = cache_keys.shape[1]
    local_width = cache_keys.shape[2]
    head_size = D // HEADS
    local_heads = local_width // head_size
    score_scale = 1.0 / math.sqrt(head_size)
    shard_index = lax.axis_index("seq")
    slot_ids = shard_index * slot_count + jnp.arange(slot_count, dtype=jnp.int32)
    live_slots = slot_ids[None, :] < lengths[:, None]
    old_keys = cache_keys.reshape(requests, slot_count, local_heads, head_size)
    old_values = cache_values.reshape(requests, slot_count, local_heads, head_size).astype(
        jnp.float32
    )
    positions = lengths[:, None] + jnp.arange(token_count, dtype=jnp.int32)[None, :]
    out_list = []
    key_list = []
    value_list = []
    for token_step in range(1):
        row_block = hidden_in
        block_rows = row_block.shape[1]
        widened = row_block.astype(jnp.float32)
        row_sums, square_sums = lax.psum(
            (jnp.sum(widened, axis=-1), jnp.sum(widened * widened, axis=-1)), "seq"
        )
        normed = normalize(widened, row_sums, square_sums)
        query_part = jnp.einsum(
            "rnc,cm->rnm", normed, query_weight, preferred_element_type=jnp.float32
        )
        key_part = jnp.einsum("rnc,cm->rnm", normed, key_weight, preferred_element_type=jnp.float32)
        value_part = jnp.einsum(
            "rnc,cm->rnm", normed, value_weight, preferred_element_type=jnp.float32
        )
        queries, keys_full, values_full = lax.psum((query_part, key_part, value_part), "seq")
        placed_pos = positions[:, token_step : token_step + block_rows]
        queries = rotate(
            queries.reshape(requests, block_rows, local_heads, head_size), placed_pos
        ).astype(jnp.bfloat16)
        new_key = rotate(
            keys_full.reshape(requests, block_rows, local_heads, head_size), placed_pos
        ).astype(jnp.bfloat16)
        new_value = values_full.reshape(requests, block_rows, local_heads, head_size).astype(
            jnp.bfloat16
        )
        keys_new = jnp.concatenate(key_list + [new_key], axis=1)
        values_new = jnp.concatenate(value_list + [new_value], axis=1)
        old_scores = (
            jnp.einsum("rnhd,rjhd->rnhj", queries, old_keys, preferred_element_type=jnp.float32)
            * score_scale
        )
        old_scores = jnp.where(live_slots[:, None, None, :], old_scores, NEGATIVE)
        top_old = jnp.max(old_scores, axis=-1)
        weights_old = jnp.where(
            live_slots[:, None, None, :], jnp.exp(old_scores - top_old[..., None]), 0.0
        )
        total_old = jnp.sum(weights_old, axis=-1)
        summed_old = jnp.einsum(
            "rnhj,rjhd->rnhd", weights_old, old_values, precision=lax.Precision.HIGHEST
        )
        top_cache = lax.pmax(top_old, "seq")
        factor_old = jnp.exp(top_old - top_cache)
        total_cache, summed_cache = lax.psum(
            (total_old * factor_old, summed_old * factor_old[..., None]), "seq"
        )
        new_scores = (
            jnp.einsum("rnhd,rshd->rnhs", queries, keys_new, preferred_element_type=jnp.float32)
            * score_scale
        )
        key_index = jnp.arange(keys_new.shape[1], dtype=jnp.int32)
        query_index = token_step + jnp.arange(block_rows, dtype=jnp.int32)
        allowed = key_index[None, :] <= query_index[:, None]
        new_scores = jnp.where(allowed[None, :, None, :], new_scores, NEGATIVE)
        top_new = jnp.max(new_scores, axis=-1)
        weights_new = jnp.exp(new_scores - top_new[..., None])
        total_new = jnp.sum(weights_new, axis=-1)
        summed_new = jnp.einsum(
            "rnhs,rshd->rnhd",
            weights_new,
            values_new.astype(jnp.float32),
            precision=lax.Precision.HIGHEST,
        )
        top_score = jnp.maximum(top_cache, top_new)
        factor_cache = jnp.exp(top_cache - top_score)
        factor_new = jnp.exp(top_new - top_score)
        running = total_cache * factor_cache + total_new * factor_new
        combined = summed_cache * factor_cache[..., None] + summed_new * factor_new[..., None]
        attended = (
            (combined / running[..., None])
            .astype(jnp.bfloat16)
            .reshape(requests, block_rows, local_width)
        )
        attn_part = jnp.einsum(
            "rnm,mc->rnc", attended, out_weight, preferred_element_type=jnp.float32
        )
        mixed = widened + lax.psum(attn_part, "mdl")
        sums_mixed, squares_mixed = lax.psum(
            (jnp.sum(mixed, axis=-1), jnp.sum(mixed * mixed, axis=-1)), "seq"
        )
        normed2 = normalize(mixed, sums_mixed, squares_mixed)
        gate_part = jnp.einsum(
            "rnc,cf->rnf", normed2, gate_weight, preferred_element_type=jnp.float32
        )
        up_part = jnp.einsum("rnc,cf->rnf", normed2, up_weight, preferred_element_type=jnp.float32)
        gate_full, up_full = lax.psum((gate_part, up_part), "seq")
        act_full = (jax.nn.silu(gate_full) * up_full).astype(jnp.bfloat16)
        down_part = jnp.einsum(
            "rnf,fc->rnc", act_full, down_weight, preferred_element_type=jnp.float32
        )
        block_out = (mixed + lax.psum(down_part, "mdl")).astype(jnp.bfloat16)
        block_out, new_key, new_value = (block_out, new_key, new_value)
        out_list.append(block_out)
        key_list.append(new_key)
        value_list.append(new_value)
    hidden_out = jnp.concatenate(out_list, axis=1)
    keys_all = jnp.concatenate(key_list, axis=1)
    values_all = jnp.concatenate(value_list, axis=1)
    slot_hits = slot_ids[None, None, :] == positions[:, :, None]
    one_hot = slot_hits.astype(jnp.bfloat16)
    written = jnp.any(slot_hits, axis=1)[..., None]
    placed_keys = jnp.einsum(
        "rts,rtm->rsm",
        one_hot,
        keys_all.reshape(requests, token_count, local_width),
        preferred_element_type=jnp.float32,
    ).astype(jnp.bfloat16)
    placed_values = jnp.einsum(
        "rts,rtm->rsm",
        one_hot,
        values_all.reshape(requests, token_count, local_width),
        preferred_element_type=jnp.float32,
    ).astype(jnp.bfloat16)
    new_cache_keys = jnp.where(written, placed_keys, cache_keys)
    new_cache_values = jnp.where(written, placed_values, cache_values)
    return (hidden_out, new_cache_keys, new_cache_values)


PLANE = 4
MESH = pl.DeviceIdType.MESH
F32 = jnp.float32
BF16 = jnp.bfloat16


def plane_peer(me, j):
    p = me % PLANE
    x, y = p % 2, p // 2
    if j % 2:
        x = 1 - x
    if j // 2:
        y = 1 - y
    return (me // PLANE) * PLANE + y * 2 + x


def depth_peer(me, k, depth):
    return ((me // PLANE + k) % depth) * PLANE + me % PLANE


def remote(src, dst, send, recv, device):
    copy = pltpu.make_async_remote_copy(
        src_ref=src, dst_ref=dst, send_sem=send, recv_sem=recv, device_id=device, device_id_type=MESH
    )
    copy.start()
    return copy


def wait_all(copies):
    for copy in copies:
        copy.wait()


def enter(n, me, partner=None):
    barrier = pltpu.get_barrier_semaphore()
    for k in range(1, n):
        pl.semaphore_signal(
            barrier, inc=1, device_id={"seq": (me + k) % n}, device_id_type=MESH
        )
    if partner is not None:
        pl.semaphore_signal(barrier, inc=1, device_id={"mdl": partner}, device_id_type=MESH)
    pl.semaphore_wait(barrier, n - 1 + (partner is not None))


def share_small(n, me, slots, send, recv):
    wait_all(
        [
            remote(
                slots.at[me], slots.at[me], send.at[k - 1], recv.at[k - 1], {"seq": (me + k) % n}
            )
            for k in range(1, n)
        ]
    )


def pipeline(
    n, me, fill, launched, finish, consume, part, got_plane, half, got_depth, whole, *sems
):
    depth = n // PLANE
    chunks = part.shape[0]
    z, p = me // PLANE, me % PLANE
    flying = {}

    def send(kind, c, src, dst, pair_at, device):
        flying.setdefault((kind, c), []).append(
            remote(src, dst, sems[2 * kind].at[pair_at], sems[2 * kind + 1].at[pair_at], {"seq": device})
        )

    for c in range(chunks):
        fill(c)
        for j in range(1, PLANE):
            peer = plane_peer(me, j)
            send(
                0,
                c,
                part.at[c, :, peer % PLANE],
                got_plane.at[c, j - 1],
                c * (PLANE - 1) + j - 1,
                peer,
            )
    launched()
    for step in range(chunks + 3):
        c = step
        if c < chunks:
            wait_all(flying[0, c])
            for d in range(depth):
                total = part[c, d, p].astype(F32)
                for j in range(PLANE - 1):
                    total = total + got_plane[c, j, d].astype(F32)
                half[c, d] = total.astype(half.dtype)
            for k in range(1, depth):
                peer = depth_peer(me, k, depth)
                send(
                    1,
                    c,
                    half.at[c, peer // PLANE],
                    got_depth.at[c, k - 1],
                    c * (depth - 1) + k - 1,
                    peer,
                )
        c = step - 1
        if 0 <= c < chunks:
            wait_all(flying[1, c])
            total = half[c, z].astype(F32)
            for k in range(depth - 1):
                total = total + got_depth[c, k].astype(F32)
            finish(c, total)
            for k in range(1, depth):
                mine = whole.at[c, z, p]
                send(
                    2, c, mine, mine, c * (depth - 1) + k - 1, depth_peer(me, k, depth)
                )
        c = step - 2
        if 0 <= c < chunks:
            wait_all(flying[2, c])
            for j in range(1, PLANE):
                mine = whole.at[c, :, p]
                send(3, c, mine, mine, c * (PLANE - 1) + j - 1, plane_peer(me, j))
        c = step - 3
        if 0 <= c < chunks:
            wait_all(flying[3, c])
            consume(c)


def row_stats(n, me, widened, slots, send, recv):
    rows = widened.shape[0]
    lanes = lax.broadcasted_iota(jnp.int32, (rows, 128), 1)
    first = jnp.sum(widened, axis=-1, keepdims=True)
    second = jnp.sum(widened * widened, axis=-1, keepdims=True)
    packed = jnp.where(lanes == 0, first, jnp.where(lanes == 1, second, 0.0))
    slots[me] = packed.T[0:8]
    share_small(n, me, slots, send, recv)
    total = slots[0]
    for i in range(1, n):
        total = total + slots[i]
    back = jnp.concatenate([total, jnp.zeros((120, rows), F32)], axis=0).T
    return back[:, 0:1], back[:, 1:2]


def normalize_rows(widened, first, second):
    mean = first / D
    inverse = 1.0 / jnp.sqrt(second / D - mean * mean + EPS)
    return ((widened - mean) * inverse).astype(BF16)


def project_kernel(
    n, x_ref, wq, wk, wv, cos_ref, sin_ref, whole, own, held, arrived, slots, send, recv, *rest
):
    me = lax.axis_index("seq")
    loads = [
        pltpu.make_async_copy(w, held.at[i], arrived.at[i]) for i, w in enumerate((wq, wk, wv))
    ]
    for load in loads:
        load.start()
    enter(n, me)
    part, got_plane, half, got_depth = rest[:4]
    widened = x_ref[...].astype(F32)
    normed = normalize_rows(widened, *row_stats(n, me, widened, slots, send, recv))
    z, p = me // PLANE, me % PLANE

    def fill(c):
        loads[c].wait()
        made = jnp.dot(normed, held[c], preferred_element_type=F32)
        part[c] = made.reshape(part.shape[1:])

    def finish(c, sums):
        for i in range(sums.shape[1] // 128):
            piece = sums[:, i * 128 : (i + 1) * 128]
            if c < 2:
                piece = piece * cos_ref[me] + pltpu.roll(piece, 64, 1) * sin_ref[me]
            piece = piece.astype(BF16)
            whole[c, z, p, :, i * 128 : (i + 1) * 128] = piece
            own[c, :, i * 128 : (i + 1) * 128] = piece

    pipeline(
        n,
        me,
        fill,
        lambda: None,
        finish,
        lambda c: None,
        part,
        got_plane,
        half,
        got_depth,
        whole,
        *rest[4:],
    )


def cache_kernel(scale, len_ref, new_ref, k_ref, v_ref, stat_ref, acc_ref, ko_ref, vo_ref):
    step = pl.program_id(0)
    group, slots, width = k_ref.shape
    base = lax.axis_index("seq") * slots
    head_mask = lax.broadcasted_iota(jnp.int32, (8, width), 1) // 128 == (
        lax.broadcasted_iota(jnp.int32, (8, width), 0)
    )
    slot = base + lax.broadcasted_iota(jnp.int32, (32, slots), 1)
    sub = lax.broadcasted_iota(jnp.int32, (8, 128), 0)
    lane = lax.broadcasted_iota(jnp.int32, (8, 128), 1)
    for i in range(group):
        length = len_ref[step * group + i]
        at = (i % 2) * 4
        fresh = new_ref[0, i // 2].astype(F32)
        keys, values = k_ref[i], v_ref[i]
        queries = jnp.concatenate(
            [jnp.where(head_mask, fresh[at + t : at + t + 1], 0.0) for t in range(4)], axis=0
        ).astype(BF16)
        scores = (
            lax.dot_general(queries, keys, (((1,), (1,)), ((), ())), preferred_element_type=F32)
            * scale
        )
        live = slot < length
        scores = jnp.where(live, scores, NEGATIVE)
        top = jnp.max(scores, axis=-1, keepdims=True)
        weights = jnp.where(live, jnp.exp(scores - top), 0.0)
        total = jnp.sum(weights, axis=-1, keepdims=True)
        coarse = weights.astype(BF16)
        fine = (weights - coarse.astype(F32)).astype(BF16)
        summed = jnp.dot(coarse, values, preferred_element_type=F32) + jnp.dot(
            fine, values, preferred_element_type=F32
        )
        for t in range(4):
            row = i * 4 + t
            part = slice(8 * t, 8 * t + 8)
            acc_ref[row : row + 1] = jnp.sum(
                jnp.where(head_mask, summed[part], 0.0), axis=0, keepdims=True
            )
            stat_ref[row : row + 1] = jnp.sum(
                jnp.where(
                    lane == sub, top[part], jnp.where(lane == sub + 8, total[part], 0.0)
                ),
                axis=0,
                keepdims=True,
            )
    for i in range(group):
        ko_ref[i] = k_ref[i]
        vo_ref[i] = v_ref[i]
    for i in range(group):
        first = len_ref[step * group + i] - base
        at = (i % 2) * 4

        @pl.when((first < slots) & (first > -4))
        def _():
            place = lax.broadcasted_iota(jnp.int32, (slots, width), 0)
            for c, old, out in ((1, k_ref, ko_ref), (2, v_ref, vo_ref)):
                rows = new_ref[c, i // 2].astype(F32)
                held = old[i].astype(F32)
                for t in range(4):
                    held = jnp.where(place == first + t, rows[at + t : at + t + 1], held)
                out[i] = held.astype(BF16)


def layer_kernel(
    n,
    scale,
    stat_ref,
    acc_ref,
    own_ref,
    x_ref,
    w_ref,
    wd,
    wg,
    wu,
    out_ref,
    tops,
    slots,
    back_ref,
    mine,
    other,
    top_send,
    top_recv,
    send,
    recv,
    swap_send,
    swap_recv,
    mixed_ref,
    weights,
    load_sem,
    weight_send,
    weight_recv,
    normed_all,
    normed_send,
    normed_recv,
    *rest,
):
    me = lax.axis_index("seq")
    partner = 1 - lax.axis_index("mdl")
    enter(n, me, partner)
    rest, feed = rest[:13], rest[13:]
    part, got_plane, half, got_depth, whole = rest[:5]
    rows = stat_ref.shape[0]
    moves = []

    def share_weights():
        wide = weights.shape[-1]

        def columns(w, q):
            return w.at[:, pl.ds(pl.multiple_of(q * wide, wide), wide)]

        for j in range(1, PLANE):
            peer = plane_peer(me, j)
            for i, w in enumerate((wg, wu)):
                at = 2 * (j - 1) + i
                moves.append(
                    remote(
                        columns(w, peer % PLANE),
                        weights.at[me % PLANE, i],
                        weight_send.at[at],
                        weight_recv.at[at],
                        {"seq": peer},
                    )
                )
        for i, w in enumerate((wg, wu)):
            load = pltpu.make_async_copy(
                columns(w, me % PLANE), weights.at[me % PLANE, i], load_sem.at[i]
            )
            load.start()
            moves.append(load)

    heads = acc_ref.shape[1] // 128
    chunks = part.shape[0]
    each = heads // chunks
    stat = stat_ref[...]
    tops[me] = stat.T[0:8]
    share_small(n, me, tops, top_send, top_recv)
    top = tops[0]
    for i in range(1, n):
        top = jnp.maximum(top, tops[i])
    back = jnp.concatenate([top, jnp.zeros((120, rows), F32)], axis=0).T
    back_ref[...] = back.reshape(back_ref.shape)
    factor = jnp.exp(stat - back)
    shape = part.shape[1:4] + (128,)
    lanes = lax.broadcasted_iota(jnp.int32, (rows, 128), 1)
    totals = jnp.where(lanes < heads, pltpu.roll(stat, 128 - heads, 1) * factor, 0.0)
    z, p = me // PLANE, me % PLANE
    top_own = back_ref[me]
    token = lax.broadcasted_iota(jnp.int32, (8, 8), 0)
    key = lax.broadcasted_iota(jnp.int32, (8, 8), 1)
    allowed = (token // 4 == key // 4) & (key <= token)

    def fill(c):
        for i in range(each):
            h = c * each + i
            part[c, :, :, :, i * 128 : (i + 1) * 128] = (
                acc_ref[:, h * 128 : (h + 1) * 128] * factor[:, h : h + 1]
            ).reshape(shape)
        part[c, :, :, :, each * 128 :] = totals.reshape(shape)

    def finish(c, sums):
        for i in range(each):
            h = c * each + i
            cols = slice(h * 128, (h + 1) * 128)
            query, keys, values = own_ref[0, :, cols], own_ref[1, :, cols], own_ref[2, :, cols]
            scores = (
                lax.dot_general(query, keys, (((1,), (1,)), ((), ())), preferred_element_type=F32)
                * scale
            )
            scores = jnp.where(allowed, scores, NEGATIVE)
            top_cache = top_own[:, h : h + 1]
            top_all = jnp.maximum(top_cache, jnp.max(scores, axis=-1, keepdims=True))
            weights = jnp.where(allowed, jnp.exp(scores - top_all), 0.0)
            kept = jnp.exp(top_cache - top_all)
            at = each * 128 + h
            running = sums[:, at : at + 1] * kept + jnp.sum(weights, axis=-1, keepdims=True)
            summed = sums[:, i * 128 : (i + 1) * 128] * kept + jnp.dot(
                weights,
                values.astype(F32),
                precision=lax.Precision.HIGHEST,
                preferred_element_type=F32,
            )
            whole[c, z, p, :, i * 128 : (i + 1) * 128] = (summed / running).astype(BF16)

    def consume(c):
        width = each * 128
        attended = whole[c].astype(F32).reshape(rows, width).astype(BF16)
        made = jnp.dot(
            attended, w_ref[c * width : (c + 1) * width], preferred_element_type=F32
        )
        mine[...] = made if c == 0 else mine[...] + made

    pipeline(n, me, fill, share_weights, finish, consume, *rest)
    remote(mine, other.at[0], swap_send.at[0], swap_recv.at[0], {"mdl": partner}).wait()
    mixed = x_ref[...].astype(F32) + (mine[...] + other[0])
    mixed_ref[...] = mixed
    normed_all[p] = normalize_rows(mixed, *row_stats(n, me, mixed, slots, send, recv))
    wait_all(
        [
            remote(
                normed_all.at[p],
                normed_all.at[p],
                normed_send.at[j - 1],
                normed_recv.at[j - 1],
                {"seq": plane_peer(me, j)},
            )
            for j in range(1, PLANE)
        ]
    )
    wait_all(moves)
    feed_forward(n, me, normed_all, weights, wd, mine, *feed)
    remote(mine, other.at[1], swap_send.at[1], swap_recv.at[1], {"mdl": partner}).wait()
    out_ref[...] = (mixed_ref[...] + (mine[...] + other[1])).astype(BF16)


def feed_forward(n, me, normed_all, weights, wd, total, part, got, whole, *sems):
    depth = n // PLANE
    z, p = me // PLANE, me % PLANE
    chunks = part.shape[0]
    wide = weights.shape[-1]
    tile = wide // chunks
    rows = normed_all.shape[1]
    flying = {}

    def send(kind, c, src, dst, pair_at, peer):
        flying.setdefault((kind, c), []).append(
            remote(src, dst, sems[2 * kind].at[pair_at], sems[2 * kind + 1].at[pair_at], {"seq": peer})
        )

    for c in range(chunks):
        for i in range(2):
            made = jnp.zeros((rows, tile), F32)
            for q in range(PLANE):
                made = made + jnp.dot(
                    normed_all[q],
                    weights[q, i, :, c * tile : (c + 1) * tile],
                    preferred_element_type=F32,
                )
            part[c, :, :, i * tile : (i + 1) * tile] = made.astype(part.dtype).reshape(
                depth, rows // depth, tile
            )
        for k in range(1, depth):
            peer = depth_peer(me, k, depth)
            send(
                0, c, part.at[c, peer // PLANE], got.at[c, k - 1], c * (depth - 1) + k - 1, peer
            )
    for step in range(chunks + 2):
        c = step
        if c < chunks:
            wait_all(flying[0, c])
            sums = part[c, z].astype(F32)
            for k in range(depth - 1):
                sums = sums + got[c, k].astype(F32)
            gate, up = sums[:, :tile], sums[:, tile:]
            whole[c, p, z] = (gate / (1.0 + jnp.exp(-gate)) * up).astype(BF16)
            mine = whole.at[c, p, z]
            for k in range(1, depth):
                send(1, c, mine, mine, c * (depth - 1) + k - 1, depth_peer(me, k, depth))
        c = step - 1
        if 0 <= c < chunks:
            wait_all(flying[1, c])
            mine = whole.at[c, p]
            for j in range(1, PLANE):
                send(2, c, mine, mine, c * (PLANE - 1) + j - 1, plane_peer(me, j))
        c = step - 2
        if 0 <= c < chunks:
            wait_all(flying[2, c])
            for q in range(PLANE):
                made = jnp.dot(
                    whole[c, q].reshape(rows, tile),
                    wd[q * wide + c * tile : q * wide + (c + 1) * tile],
                    preferred_element_type=F32,
                )
                total[...] = made if c == 0 and q == 0 else total[...] + made


def pair(count):
    return [pltpu.SemaphoreType.DMA((count,))] * 2


def call(kernel, identity, outs, scratch, *operands, far=()):
    vmem = pl.BlockSpec(memory_space=pltpu.VMEM)
    return pl.pallas_call(
        kernel,
        out_shape=outs,
        in_specs=[
            pl.BlockSpec(memory_space=pl.ANY) if i in far else vmem for i in range(len(operands))
        ],
        out_specs=[vmem] * len(outs),
        scratch_shapes=scratch,
        compiler_params=pltpu.CompilerParams(
            collective_id=identity, has_side_effects=True, vmem_limit_bytes=48 * 2**20
        ),
    )(*operands)


def sum_scratch(chunks, depth, width, dtype):
    return [
        pltpu.VMEM((chunks, depth, PLANE, 8, width), dtype),
        pltpu.VMEM((chunks, PLANE - 1, depth, 8, width), dtype),
        pltpu.VMEM((chunks, depth, 8, width), dtype),
        pltpu.VMEM((chunks, depth - 1, 8, width), dtype),
    ]


def pipe_sems(chunks, depth):
    plane, line = pair(chunks * (PLANE - 1)), pair(chunks * (depth - 1))
    return plane + line + line + plane


def body_kernels(
    n,
    hidden_in,
    cache_keys,
    cache_values,
    lengths,
    query_weight,
    key_weight,
    value_weight,
    out_weight,
    gate_weight,
    up_weight,
    down_weight,
):
    requests, token_count, narrow = hidden_in.shape
    rows = requests * token_count
    depth = n // PLANE
    slot_count, local_width = cache_keys.shape[1:]
    head_size = D // HEADS
    score_scale = 1.0 / math.sqrt(head_size)
    positions = lengths[:, None] + jnp.arange(token_count, dtype=jnp.int32)[None, :]
    half_dim = head_size // 2
    freqs = THETA ** (-jnp.arange(half_dim, dtype=F32) * 2.0 / head_size)
    angles = positions.reshape(rows, 1).astype(F32) * freqs
    cosine, sine = jnp.cos(angles), jnp.sin(angles)
    cosine = jnp.concatenate([cosine, cosine], axis=-1).reshape(n, 8, head_size)
    sine = jnp.concatenate([-sine, sine], axis=-1).reshape(n, 8, head_size)
    x = hidden_in.reshape(rows, narrow)
    struct = jax.ShapeDtypeStruct
    whole, own = call(
        functools.partial(project_kernel, n),
        1,
        [struct((3, depth, PLANE, 8, local_width), BF16), struct((3, 8, local_width), BF16)],
        [
            pltpu.VMEM((3, narrow, local_width), BF16),
            pltpu.SemaphoreType.DMA((3,)),
            pltpu.VMEM((n, 8, 128), F32),
        ]
        + pair(n - 1)
        + sum_scratch(3, depth, local_width, F32)
        + pipe_sems(3, depth),
        x,
        query_weight,
        key_weight,
        value_weight,
        cosine,
        sine,
        far=(1, 2, 3),
    )
    group = 4
    block = pl.BlockSpec((group, slot_count, local_width), lambda g: (g, 0, 0))
    stat, acc, new_keys, new_values = pl.pallas_call(
        functools.partial(cache_kernel, score_scale),
        grid=(requests // group,),
        out_shape=[
            struct((rows, 128), F32),
            struct((rows, local_width), F32),
            struct(cache_keys.shape, BF16),
            struct(cache_values.shape, BF16),
        ],
        in_specs=[
            pl.BlockSpec(memory_space=pltpu.SMEM),
            pl.BlockSpec((3, group // 2, 8, local_width), lambda g: (0, g, 0, 0)),
            block,
            block,
        ],
        out_specs=[
            pl.BlockSpec((group * 4, 128), lambda g: (g, 0)),
            pl.BlockSpec((group * 4, local_width), lambda g: (g, 0)),
            block,
            block,
        ],
    )(lengths, whole.reshape(3, n, 8, local_width), cache_keys, cache_values)
    wide = gate_weight.shape[1] // PLANE
    chunks = wide // 256
    (block_out,) = call(
        functools.partial(layer_kernel, n, score_scale),
        2,
        [struct((rows, narrow), BF16)],
        [
            pltpu.VMEM((n, 8, 128), F32),
            pltpu.VMEM((n, 8, 128), F32),
            pltpu.VMEM((n, 8, 128), F32),
            pltpu.VMEM((rows, narrow), F32),
            pltpu.VMEM((2, rows, narrow), F32),
        ]
        + pair(n - 1)
        + pair(n - 1)
        + pair(2)
        + [
            pltpu.VMEM((rows, narrow), F32),
            pltpu.VMEM((PLANE, 2, narrow, wide), BF16),
            pltpu.SemaphoreType.DMA((2,)),
        ]
        + pair(2 * (PLANE - 1))
        + [pltpu.VMEM((PLANE, rows, narrow), BF16)]
        + pair(PLANE - 1)
        + sum_scratch(2, depth, local_width // 2 + 128, F32)
        + [pltpu.VMEM((2, depth, PLANE, 8, local_width // 2), BF16)]
        + pipe_sems(2, depth)
        + [
            pltpu.VMEM((chunks, depth, rows // depth, 512), BF16),
            pltpu.VMEM((chunks, depth - 1, rows // depth, 512), BF16),
            pltpu.VMEM((chunks, PLANE, depth, rows // depth, 256), BF16),
        ]
        + pair(chunks * (depth - 1))
        + pair(chunks * (depth - 1))
        + pair(chunks * (PLANE - 1)),
        stat,
        acc,
        own,
        x,
        out_weight,
        down_weight,
        gate_weight,
        up_weight,
        far=(6, 7),
    )
    return block_out.reshape(requests, token_count, narrow), new_keys, new_values


def body(n, model_shards, hidden_in, cache_keys, *rest):
    rows = hidden_in.shape[0] * hidden_in.shape[1]
    tiled = (
        n % PLANE == 0
        and rows == 128
        and rows // n == 8
        and hidden_in.shape[1] == 4
        and hidden_in.shape[2] == 128
        and cache_keys.shape[2] == 1024
        and model_shards == 2
    )
    if tiled:
        return body_kernels(n, hidden_in, cache_keys, *rest)
    return body_plain(hidden_in, cache_keys, *rest)


def solution(mesh):
    placed = (
        P(None, None, "seq"),
        P(None, "seq", "mdl"),
        P(None, "seq", "mdl"),
        P(),
        P("seq", "mdl"),
        P("seq", "mdl"),
        P("seq", "mdl"),
        P("mdl", "seq"),
        P("seq", "mdl"),
        P("seq", "mdl"),
        P("mdl", "seq"),
    )
    return jax.shard_map(
        functools.partial(body, mesh.shape["seq"], mesh.shape["mdl"]),
        mesh=mesh,
        in_specs=placed,
        out_specs=(P(None, None, "seq"), P(None, "seq", "mdl"), P(None, "seq", "mdl")),
        check_vma=False,
    )
```

```python
import functools
import math

import jax
import jax.numpy as jnp
from jax import lax
from jax.experimental import pallas as pl
from jax.experimental.pallas import tpu as pltpu
from jax.sharding import PartitionSpec as P

D = 2048
HEADS = 16


EPS = 1e-05
THETA = 10000.0
NEGATIVE = -1e30


def rotate(vectors, placed_pos):
    head_size = vectors.shape[-1]
    half_dim = head_size // 2
    freqs = THETA ** (-jnp.arange(half_dim, dtype=jnp.float32) * 2.0 / head_size)
    angles = placed_pos.astype(jnp.float32)[..., None, None] * freqs
    cosine = jnp.cos(angles)
    sine = jnp.sin(angles)
    first_half = vectors[..., :half_dim]
    second_half = vectors[..., half_dim:]
    return jnp.concatenate(
        [first_half * cosine - second_half * sine, second_half * cosine + first_half * sine],
        axis=-1,
    )


def normalize(widened, row_sums, square_sums):
    row_mean = row_sums / D
    second_moment = square_sums / D
    inverse = 1.0 / jnp.sqrt(second_moment - row_mean * row_mean + EPS)
    return ((widened - row_mean[..., None]) * inverse[..., None]).astype(jnp.bfloat16)


def body_plain(
    hidden_in,
    cache_keys,
    cache_values,
    lengths,
    query_weight,
    key_weight,
    value_weight,
    out_weight,
    gate_weight,
    up_weight,
    down_weight,
):
    requests, token_count, narrow_width = hidden_in.shape
    slot_count = cache_keys.shape[1]
    local_width = cache_keys.shape[2]
    head_size = D // HEADS
    local_heads = local_width // head_size
    score_scale = 1.0 / math.sqrt(head_size)
    shard_index = lax.axis_index("seq")
    slot_ids = shard_index * slot_count + jnp.arange(slot_count, dtype=jnp.int32)
    live_slots = slot_ids[None, :] < lengths[:, None]
    old_keys = cache_keys.reshape(requests, slot_count, local_heads, head_size)
    old_values = cache_values.reshape(requests, slot_count, local_heads, head_size).astype(
        jnp.float32
    )
    positions = lengths[:, None] + jnp.arange(token_count, dtype=jnp.int32)[None, :]
    out_list = []
    key_list = []
    value_list = []
    for token_step in range(1):
        row_block = hidden_in
        block_rows = row_block.shape[1]
        widened = row_block.astype(jnp.float32)
        row_sums, square_sums = lax.psum(
            (jnp.sum(widened, axis=-1), jnp.sum(widened * widened, axis=-1)), "seq"
        )
        normed = normalize(widened, row_sums, square_sums)
        query_part = jnp.einsum(
            "rnc,cm->rnm", normed, query_weight, preferred_element_type=jnp.float32
        )
        key_part = jnp.einsum("rnc,cm->rnm", normed, key_weight, preferred_element_type=jnp.float32)
        value_part = jnp.einsum(
            "rnc,cm->rnm", normed, value_weight, preferred_element_type=jnp.float32
        )
        queries, keys_full, values_full = lax.psum((query_part, key_part, value_part), "seq")
        placed_pos = positions[:, token_step : token_step + block_rows]
        queries = rotate(
            queries.reshape(requests, block_rows, local_heads, head_size), placed_pos
        ).astype(jnp.bfloat16)
        new_key = rotate(
            keys_full.reshape(requests, block_rows, local_heads, head_size), placed_pos
        ).astype(jnp.bfloat16)
        new_value = values_full.reshape(requests, block_rows, local_heads, head_size).astype(
            jnp.bfloat16
        )
        keys_new = jnp.concatenate(key_list + [new_key], axis=1)
        values_new = jnp.concatenate(value_list + [new_value], axis=1)
        old_scores = (
            jnp.einsum("rnhd,rjhd->rnhj", queries, old_keys, preferred_element_type=jnp.float32)
            * score_scale
        )
        old_scores = jnp.where(live_slots[:, None, None, :], old_scores, NEGATIVE)
        top_old = jnp.max(old_scores, axis=-1)
        weights_old = jnp.where(
            live_slots[:, None, None, :], jnp.exp(old_scores - top_old[..., None]), 0.0
        )
        total_old = jnp.sum(weights_old, axis=-1)
        summed_old = jnp.einsum(
            "rnhj,rjhd->rnhd", weights_old, old_values, precision=lax.Precision.HIGHEST
        )
        top_cache = lax.pmax(top_old, "seq")
        factor_old = jnp.exp(top_old - top_cache)
        total_cache, summed_cache = lax.psum(
            (total_old * factor_old, summed_old * factor_old[..., None]), "seq"
        )
        new_scores = (
            jnp.einsum("rnhd,rshd->rnhs", queries, keys_new, preferred_element_type=jnp.float32)
            * score_scale
        )
        key_index = jnp.arange(keys_new.shape[1], dtype=jnp.int32)
        query_index = token_step + jnp.arange(block_rows, dtype=jnp.int32)
        allowed = key_index[None, :] <= query_index[:, None]
        new_scores = jnp.where(allowed[None, :, None, :], new_scores, NEGATIVE)
        top_new = jnp.max(new_scores, axis=-1)
        weights_new = jnp.exp(new_scores - top_new[..., None])
        total_new = jnp.sum(weights_new, axis=-1)
        summed_new = jnp.einsum(
            "rnhs,rshd->rnhd",
            weights_new,
            values_new.astype(jnp.float32),
            precision=lax.Precision.HIGHEST,
        )
        top_score = jnp.maximum(top_cache, top_new)
        factor_cache = jnp.exp(top_cache - top_score)
        factor_new = jnp.exp(top_new - top_score)
        running = total_cache * factor_cache + total_new * factor_new
        combined = summed_cache * factor_cache[..., None] + summed_new * factor_new[..., None]
        attended = (
            (combined / running[..., None])
            .astype(jnp.bfloat16)
            .reshape(requests, block_rows, local_width)
        )
        attn_part = jnp.einsum(
            "rnm,mc->rnc", attended, out_weight, preferred_element_type=jnp.float32
        )
        mixed = widened + lax.psum(attn_part, "mdl")
        sums_mixed, squares_mixed = lax.psum(
            (jnp.sum(mixed, axis=-1), jnp.sum(mixed * mixed, axis=-1)), "seq"
        )
        normed2 = normalize(mixed, sums_mixed, squares_mixed)
        gate_part = jnp.einsum(
            "rnc,cf->rnf", normed2, gate_weight, preferred_element_type=jnp.float32
        )
        up_part = jnp.einsum("rnc,cf->rnf", normed2, up_weight, preferred_element_type=jnp.float32)
        gate_full, up_full = lax.psum((gate_part, up_part), "seq")
        act_full = (jax.nn.silu(gate_full) * up_full).astype(jnp.bfloat16)
        down_part = jnp.einsum(
            "rnf,fc->rnc", act_full, down_weight, preferred_element_type=jnp.float32
        )
        block_out = (mixed + lax.psum(down_part, "mdl")).astype(jnp.bfloat16)
        block_out, new_key, new_value = (block_out, new_key, new_value)
        out_list.append(block_out)
        key_list.append(new_key)
        value_list.append(new_value)
    hidden_out = jnp.concatenate(out_list, axis=1)
    keys_all = jnp.concatenate(key_list, axis=1)
    values_all = jnp.concatenate(value_list, axis=1)
    slot_hits = slot_ids[None, None, :] == positions[:, :, None]
    one_hot = slot_hits.astype(jnp.bfloat16)
    written = jnp.any(slot_hits, axis=1)[..., None]
    placed_keys = jnp.einsum(
        "rts,rtm->rsm",
        one_hot,
        keys_all.reshape(requests, token_count, local_width),
        preferred_element_type=jnp.float32,
    ).astype(jnp.bfloat16)
    placed_values = jnp.einsum(
        "rts,rtm->rsm",
        one_hot,
        values_all.reshape(requests, token_count, local_width),
        preferred_element_type=jnp.float32,
    ).astype(jnp.bfloat16)
    new_cache_keys = jnp.where(written, placed_keys, cache_keys)
    new_cache_values = jnp.where(written, placed_values, cache_values)
    return (hidden_out, new_cache_keys, new_cache_values)


PLANE = 4
MESH = pl.DeviceIdType.MESH
F32 = jnp.float32
BF16 = jnp.bfloat16


def plane_peer(me, j):
    p = me % PLANE
    x, y = p % 2, p // 2
    if j % 2:
        x = 1 - x
    if j // 2:
        y = 1 - y
    return (me // PLANE) * PLANE + y * 2 + x


def depth_peer(me, k, depth):
    return ((me // PLANE + k) % depth) * PLANE + me % PLANE


def remote(src, dst, send, recv, device):
    copy = pltpu.make_async_remote_copy(
        src_ref=src, dst_ref=dst, send_sem=send, recv_sem=recv, device_id=device, device_id_type=MESH
    )
    copy.start()
    return copy


def wait_all(copies):
    for copy in copies:
        copy.wait()


def enter(n, me, partner=None):
    barrier = pltpu.get_barrier_semaphore()
    for k in range(1, n):
        pl.semaphore_signal(
            barrier, inc=1, device_id={"seq": (me + k) % n}, device_id_type=MESH
        )
    if partner is not None:
        pl.semaphore_signal(barrier, inc=1, device_id={"mdl": partner}, device_id_type=MESH)
    pl.semaphore_wait(barrier, n - 1 + (partner is not None))


def share_small(n, me, slots, send, recv):
    wait_all(
        [
            remote(
                slots.at[me], slots.at[me], send.at[k - 1], recv.at[k - 1], {"seq": (me + k) % n}
            )
            for k in range(1, n)
        ]
    )


def chunk(refs, c):
    return refs[c] if isinstance(refs, list) else refs.at[c]


def pipeline(
    n, me, fill, finish, consume, part, got_plane, half, got_depth, whole, *sems
):
    depth = n // PLANE
    chunks = len(part) if isinstance(part, list) else part.shape[0]
    z, p = me // PLANE, me % PLANE
    flying = {}

    def send(kind, c, src, dst, pair_at, device):
        flying.setdefault((kind, c), []).append(
            remote(src, dst, sems[2 * kind].at[pair_at], sems[2 * kind + 1].at[pair_at], {"seq": device})
        )

    for c in range(chunks):
        fill(c)
        for j in range(1, PLANE):
            peer = plane_peer(me, j)
            send(
                0,
                c,
                chunk(part, c).at[:, peer % PLANE],
                chunk(got_plane, c).at[j - 1],
                c * (PLANE - 1) + j - 1,
                peer,
            )
    for step in range(chunks + 3):
        c = step
        if c < chunks:
            wait_all(flying[0, c])
            for d in range(depth):
                total = chunk(part, c)[d, p].astype(F32)
                for j in range(PLANE - 1):
                    total = total + chunk(got_plane, c)[j, d].astype(F32)
                mine = chunk(half, c)
                mine[d] = total.astype(mine.dtype)
            for k in range(1, depth):
                peer = depth_peer(me, k, depth)
                send(
                    1,
                    c,
                    chunk(half, c).at[peer // PLANE],
                    chunk(got_depth, c).at[k - 1],
                    c * (depth - 1) + k - 1,
                    peer,
                )
        c = step - 1
        if 0 <= c < chunks:
            wait_all(flying[1, c])
            total = chunk(half, c)[z].astype(F32)
            for k in range(depth - 1):
                total = total + chunk(got_depth, c)[k].astype(F32)
            finish(c, total)
            for k in range(1, depth):
                mine = whole.at[c, z, p]
                send(
                    2, c, mine, mine, c * (depth - 1) + k - 1, depth_peer(me, k, depth)
                )
        c = step - 2
        if 0 <= c < chunks:
            wait_all(flying[2, c])
            for j in range(1, PLANE):
                mine = whole.at[c, :, p]
                send(3, c, mine, mine, c * (PLANE - 1) + j - 1, plane_peer(me, j))
        c = step - 3
        if 0 <= c < chunks:
            wait_all(flying[3, c])
            consume(c)


def row_stats(n, me, widened, slots, send, recv):
    rows = widened.shape[0]
    lanes = lax.broadcasted_iota(jnp.int32, (rows, 128), 1)
    first = jnp.sum(widened, axis=-1, keepdims=True)
    second = jnp.sum(widened * widened, axis=-1, keepdims=True)
    packed = jnp.where(lanes == 0, first, jnp.where(lanes == 1, second, 0.0))
    slots[me] = packed.T[0:8]
    share_small(n, me, slots, send, recv)
    total = slots[0]
    for i in range(1, n):
        total = total + slots[i]
    back = jnp.concatenate([total, jnp.zeros((120, rows), F32)], axis=0).T
    return back[:, 0:1], back[:, 1:2]


def normalize_rows(widened, first, second):
    mean = first / D
    inverse = 1.0 / jnp.sqrt(second / D - mean * mean + EPS)
    return ((widened - mean) * inverse).astype(BF16)


def project_kernel(
    n, x_ref, wq, wk, wv, cos_ref, sin_ref, whole, own, held, arrived, slots, send, recv, *rest
):
    me = lax.axis_index("seq")
    loads = [
        pltpu.make_async_copy(w, held.at[i], arrived.at[i]) for i, w in enumerate((wq, wk, wv))
    ]
    for load in loads:
        load.start()
    enter(n, me)
    part, got_plane, half, got_depth = (
        [rest[i], rest[4 + i].at[0], rest[4 + i].at[1]] for i in range(4)
    )
    widened = x_ref[...].astype(F32)
    normed = normalize_rows(widened, *row_stats(n, me, widened, slots, send, recv))
    z, p = me // PLANE, me % PLANE

    def fill(c):
        loads[c].wait()
        made = jnp.dot(normed, held[c], preferred_element_type=F32)
        part[c][...] = made.reshape(part[c].shape).astype(part[c].dtype)

    def finish(c, sums):
        for i in range(sums.shape[1] // 128):
            piece = sums[:, i * 128 : (i + 1) * 128]
            if c < 2:
                piece = piece * cos_ref[me] + pltpu.roll(piece, 64, 1) * sin_ref[me]
            piece = piece.astype(BF16)
            whole[c, z, p, :, i * 128 : (i + 1) * 128] = piece
            own[c, :, i * 128 : (i + 1) * 128] = piece

    pipeline(
        n, me, fill, finish, lambda c: None, part, got_plane, half, got_depth, whole, *rest[8:]
    )


def cache_kernel(scale, len_ref, new_ref, k_ref, v_ref, stat_ref, acc_ref, ko_ref, vo_ref):
    step = pl.program_id(0)
    group, slots, width = k_ref.shape
    base = lax.axis_index("seq") * slots
    head_mask = lax.broadcasted_iota(jnp.int32, (8, width), 1) // 128 == (
        lax.broadcasted_iota(jnp.int32, (8, width), 0)
    )
    slot = base + lax.broadcasted_iota(jnp.int32, (32, slots), 1)
    sub = lax.broadcasted_iota(jnp.int32, (8, 128), 0)
    lane = lax.broadcasted_iota(jnp.int32, (8, 128), 1)
    for i in range(group):
        length = len_ref[step * group + i]
        at = (i % 2) * 4
        fresh = new_ref[0, i // 2].astype(F32)
        keys, values = k_ref[i], v_ref[i]
        queries = jnp.concatenate(
            [jnp.where(head_mask, fresh[at + t : at + t + 1], 0.0) for t in range(4)], axis=0
        ).astype(BF16)
        scores = (
            lax.dot_general(queries, keys, (((1,), (1,)), ((), ())), preferred_element_type=F32)
            * scale
        )
        live = slot < length
        scores = jnp.where(live, scores, NEGATIVE)
        top = jnp.max(scores, axis=-1, keepdims=True)
        weights = jnp.where(live, jnp.exp(scores - top), 0.0)
        total = jnp.sum(weights, axis=-1, keepdims=True)
        coarse = weights.astype(BF16)
        fine = (weights - coarse.astype(F32)).astype(BF16)
        summed = jnp.dot(coarse, values, preferred_element_type=F32) + jnp.dot(
            fine, values, preferred_element_type=F32
        )
        for t in range(4):
            row = i * 4 + t
            part = slice(8 * t, 8 * t + 8)
            acc_ref[row : row + 1] = jnp.sum(
                jnp.where(head_mask, summed[part], 0.0), axis=0, keepdims=True
            )
            stat_ref[row : row + 1] = jnp.sum(
                jnp.where(
                    lane == sub, top[part], jnp.where(lane == sub + 8, total[part], 0.0)
                ),
                axis=0,
                keepdims=True,
            )
    for i in range(group):
        ko_ref[i] = k_ref[i]
        vo_ref[i] = v_ref[i]
    for i in range(group):
        first = len_ref[step * group + i] - base
        at = (i % 2) * 4

        @pl.when((first < slots) & (first > -4))
        def _():
            place = lax.broadcasted_iota(jnp.int32, (slots, width), 0)
            for c, old, out in ((1, k_ref, ko_ref), (2, v_ref, vo_ref)):
                rows = new_ref[c, i // 2].astype(F32)
                held = old[i].astype(F32)
                for t in range(4):
                    held = jnp.where(place == first + t, rows[at + t : at + t + 1], held)
                out[i] = held.astype(BF16)


def attend_kernel(
    n,
    scale,
    stat_ref,
    acc_ref,
    own_ref,
    x_ref,
    w_ref,
    mixed_ref,
    normed_ref,
    tops,
    slots,
    back_ref,
    mine,
    other,
    top_send,
    top_recv,
    send,
    recv,
    swap_send,
    swap_recv,
    *rest,
):
    me = lax.axis_index("seq")
    partner = 1 - lax.axis_index("mdl")
    enter(n, me, partner)
    part, got_plane, half, got_depth, whole = rest[:5]
    rows = stat_ref.shape[0]
    heads = acc_ref.shape[1] // 128
    chunks = part.shape[0]
    each = heads // chunks
    stat = stat_ref[...]
    tops[me] = stat.T[0:8]
    share_small(n, me, tops, top_send, top_recv)
    top = tops[0]
    for i in range(1, n):
        top = jnp.maximum(top, tops[i])
    back = jnp.concatenate([top, jnp.zeros((120, rows), F32)], axis=0).T
    back_ref[...] = back.reshape(back_ref.shape)
    factor = jnp.exp(stat - back)
    shape = part.shape[1:4] + (128,)
    lanes = lax.broadcasted_iota(jnp.int32, (rows, 128), 1)
    totals = jnp.where(lanes < heads, pltpu.roll(stat, 128 - heads, 1) * factor, 0.0)
    z, p = me // PLANE, me % PLANE
    top_own = back_ref[me]
    token = lax.broadcasted_iota(jnp.int32, (8, 8), 0)
    key = lax.broadcasted_iota(jnp.int32, (8, 8), 1)
    allowed = (token // 4 == key // 4) & (key <= token)

    def fill(c):
        for i in range(each):
            h = c * each + i
            part[c, :, :, :, i * 128 : (i + 1) * 128] = (
                acc_ref[:, h * 128 : (h + 1) * 128] * factor[:, h : h + 1]
            ).reshape(shape)
        part[c, :, :, :, each * 128 :] = totals.reshape(shape)

    def finish(c, sums):
        for i in range(each):
            h = c * each + i
            cols = slice(h * 128, (h + 1) * 128)
            query, keys, values = own_ref[0, :, cols], own_ref[1, :, cols], own_ref[2, :, cols]
            scores = (
                lax.dot_general(query, keys, (((1,), (1,)), ((), ())), preferred_element_type=F32)
                * scale
            )
            scores = jnp.where(allowed, scores, NEGATIVE)
            top_cache = top_own[:, h : h + 1]
            top_all = jnp.maximum(top_cache, jnp.max(scores, axis=-1, keepdims=True))
            weights = jnp.where(allowed, jnp.exp(scores - top_all), 0.0)
            kept = jnp.exp(top_cache - top_all)
            at = each * 128 + h
            running = sums[:, at : at + 1] * kept + jnp.sum(weights, axis=-1, keepdims=True)
            summed = sums[:, i * 128 : (i + 1) * 128] * kept + jnp.dot(
                weights,
                values.astype(F32),
                precision=lax.Precision.HIGHEST,
                preferred_element_type=F32,
            )
            whole[c, z, p, :, i * 128 : (i + 1) * 128] = (summed / running).astype(BF16)

    def consume(c):
        width = each * 128
        attended = whole[c].astype(F32).reshape(rows, width).astype(BF16)
        made = jnp.dot(
            attended, w_ref[c * width : (c + 1) * width], preferred_element_type=F32
        )
        mine[...] = made if c == 0 else mine[...] + made

    pipeline(n, me, fill, finish, consume, *rest)
    remote(mine, other, swap_send.at[0], swap_recv.at[0], {"mdl": partner}).wait()
    mixed = x_ref[...].astype(F32) + (mine[...] + other[...])
    mixed_ref[...] = mixed
    normed_ref[...] = normalize_rows(mixed, *row_stats(n, me, mixed, slots, send, recv))


def feed_kernel(
    n,
    normed_ref,
    mixed_ref,
    wg,
    wu,
    wd,
    out_ref,
    mine,
    other,
    swap_send,
    swap_recv,
    *rest,
):
    me = lax.axis_index("seq")
    partner = 1 - lax.axis_index("mdl")
    enter(n, me, partner)
    part, got_plane, half, got_depth, whole = rest[:5]
    rows = normed_ref.shape[0]
    tile = whole.shape[-1]
    normed = normed_ref[...]
    shape = part.shape[1:4] + (tile,)
    z, p = me // PLANE, me % PLANE

    def fill(c):
        for i, w in enumerate((wg, wu)):
            made = jnp.dot(
                normed, w[:, c * tile : (c + 1) * tile], preferred_element_type=F32
            )
            part[c, :, :, :, i * tile : (i + 1) * tile] = made.reshape(shape).astype(part.dtype)

    def finish(c, sums):
        gate, up = sums[:, :tile], sums[:, tile:]
        whole[c, z, p] = (gate / (1.0 + jnp.exp(-gate)) * up).astype(BF16)

    def consume(c):
        act = whole[c].astype(F32).reshape(rows, tile).astype(BF16)
        made = jnp.dot(act, wd[c * tile : (c + 1) * tile], preferred_element_type=F32)
        mine[...] = made if c == 0 else mine[...] + made

    pipeline(n, me, fill, finish, consume, *rest)
    remote(mine, other, swap_send.at[0], swap_recv.at[0], {"mdl": partner}).wait()
    out_ref[...] = (mixed_ref[...] + (mine[...] + other[...])).astype(BF16)


def pair(count):
    return [pltpu.SemaphoreType.DMA((count,))] * 2


def call(kernel, identity, outs, scratch, *operands, far=()):
    vmem = pl.BlockSpec(memory_space=pltpu.VMEM)
    return pl.pallas_call(
        kernel,
        out_shape=outs,
        in_specs=[
            pl.BlockSpec(memory_space=pl.ANY) if i in far else vmem for i in range(len(operands))
        ],
        out_specs=[vmem] * len(outs),
        scratch_shapes=scratch,
        compiler_params=pltpu.CompilerParams(
            collective_id=identity, has_side_effects=True, vmem_limit_bytes=48 * 2**20
        ),
    )(*operands)


def sum_scratch(chunks, depth, width, dtype):
    return [
        pltpu.VMEM((chunks, depth, PLANE, 8, width), dtype),
        pltpu.VMEM((chunks, PLANE - 1, depth, 8, width), dtype),
        pltpu.VMEM((chunks, depth, 8, width), dtype),
        pltpu.VMEM((chunks, depth - 1, 8, width), dtype),
    ]


def pipe_sems(chunks, depth):
    plane, line = pair(chunks * (PLANE - 1)), pair(chunks * (depth - 1))
    return plane + line + line + plane


def body_kernels(
    n,
    hidden_in,
    cache_keys,
    cache_values,
    lengths,
    query_weight,
    key_weight,
    value_weight,
    out_weight,
    gate_weight,
    up_weight,
    down_weight,
):
    requests, token_count, narrow = hidden_in.shape
    rows = requests * token_count
    depth = n // PLANE
    slot_count, local_width = cache_keys.shape[1:]
    head_size = D // HEADS
    score_scale = 1.0 / math.sqrt(head_size)
    positions = lengths[:, None] + jnp.arange(token_count, dtype=jnp.int32)[None, :]
    half_dim = head_size // 2
    freqs = THETA ** (-jnp.arange(half_dim, dtype=F32) * 2.0 / head_size)
    angles = positions.reshape(rows, 1).astype(F32) * freqs
    cosine, sine = jnp.cos(angles), jnp.sin(angles)
    cosine = jnp.concatenate([cosine, cosine], axis=-1).reshape(n, 8, head_size)
    sine = jnp.concatenate([-sine, sine], axis=-1).reshape(n, 8, head_size)
    x = hidden_in.reshape(rows, narrow)
    struct = jax.ShapeDtypeStruct
    whole, own = call(
        functools.partial(project_kernel, n),
        1,
        [struct((3, depth, PLANE, 8, local_width), BF16), struct((3, 8, local_width), BF16)],
        [
            pltpu.VMEM((3, narrow, local_width), BF16),
            pltpu.SemaphoreType.DMA((3,)),
            pltpu.VMEM((n, 8, 128), F32),
        ]
        + pair(n - 1)
        + [
            pltpu.VMEM(ref.shape[1:], F32) for ref in sum_scratch(1, depth, local_width, F32)
        ]
        + sum_scratch(2, depth, local_width, BF16)
        + pipe_sems(3, depth),
        x,
        query_weight,
        key_weight,
        value_weight,
        cosine,
        sine,
        far=(1, 2, 3),
    )
    group = 4
    block = pl.BlockSpec((group, slot_count, local_width), lambda g: (g, 0, 0))
    stat, acc, new_keys, new_values = pl.pallas_call(
        functools.partial(cache_kernel, score_scale),
        grid=(requests // group,),
        out_shape=[
            struct((rows, 128), F32),
            struct((rows, local_width), F32),
            struct(cache_keys.shape, BF16),
            struct(cache_values.shape, BF16),
        ],
        in_specs=[
            pl.BlockSpec(memory_space=pltpu.SMEM),
            pl.BlockSpec((3, group // 2, 8, local_width), lambda g: (0, g, 0, 0)),
            block,
            block,
        ],
        out_specs=[
            pl.BlockSpec((group * 4, 128), lambda g: (g, 0)),
            pl.BlockSpec((group * 4, local_width), lambda g: (g, 0)),
            block,
            block,
        ],
    )(lengths, whole.reshape(3, n, 8, local_width), cache_keys, cache_values)
    mixed, normed2 = call(
        functools.partial(attend_kernel, n, score_scale),
        2,
        [struct((rows, narrow), F32), struct((rows, narrow), BF16)],
        [
            pltpu.VMEM((n, 8, 128), F32),
            pltpu.VMEM((n, 8, 128), F32),
            pltpu.VMEM((n, 8, 128), F32),
            pltpu.VMEM((rows, narrow), F32),
            pltpu.VMEM((rows, narrow), F32),
        ]
        + pair(n - 1)
        + pair(n - 1)
        + pair(1)
        + sum_scratch(2, depth, local_width // 2 + 128, F32)
        + [pltpu.VMEM((2, depth, PLANE, 8, local_width // 2), BF16)]
        + pipe_sems(2, depth),
        stat,
        acc,
        own,
        x,
        out_weight,
    )
    ff = gate_weight.shape[1]
    chunks = ff // 1024
    (block_out,) = call(
        functools.partial(feed_kernel, n),
        3,
        [struct((rows, narrow), BF16)],
        [pltpu.VMEM((rows, narrow), F32), pltpu.VMEM((rows, narrow), F32)]
        + pair(1)
        + sum_scratch(chunks, depth, 2 * ff // chunks, BF16)
        + [pltpu.VMEM((chunks, depth, PLANE, 8, ff // chunks), BF16)]
        + pipe_sems(chunks, depth),
        normed2,
        mixed,
        gate_weight,
        up_weight,
        down_weight,
    )
    return block_out.reshape(requests, token_count, narrow), new_keys, new_values


def body(n, model_shards, hidden_in, cache_keys, *rest):
    rows = hidden_in.shape[0] * hidden_in.shape[1]
    tiled = (
        n % PLANE == 0
        and rows == 128
        and rows // n == 8
        and hidden_in.shape[1] == 4
        and hidden_in.shape[2] == 128
        and cache_keys.shape[2] == 1024
        and model_shards == 2
    )
    if tiled:
        return body_kernels(n, hidden_in, cache_keys, *rest)
    return body_plain(hidden_in, cache_keys, *rest)


def solution(mesh):
    placed = (
        P(None, None, "seq"),
        P(None, "seq", "mdl"),
        P(None, "seq", "mdl"),
        P(),
        P("seq", "mdl"),
        P("seq", "mdl"),
        P("seq", "mdl"),
        P("mdl", "seq"),
        P("seq", "mdl"),
        P("seq", "mdl"),
        P("mdl", "seq"),
    )
    return jax.shard_map(
        functools.partial(body, mesh.shape["seq"], mesh.shape["mdl"]),
        mesh=mesh,
        in_specs=placed,
        out_specs=(P(None, None, "seq"), P(None, "seq", "mdl"), P(None, "seq", "mdl")),
        check_vma=False,
    )
```
